1024 devices in a mesh: dom: 256 (over z, x, core), sub: 4 (over y).
Axes of the slice: x: 4, y: 4, z: 32, core: 2. Of those that a mesh axis runs over, the one named last changes fastest.
Arguments:
- element_load: float32 [256, 8, 32, 8, 128], P('dom', None, 'sub'), may hold values from -48 to 48
- mobility: float32 [256, 8, 32, 8, 128], P('dom', None, 'sub'), may hold values from 0.5 to 4
- metric: float32 [3, 256, 32, 16], P(None, 'dom', 'sub'), may hold values from 0.5 to 2
Outputs:
- pressure: float32 [256, 8, 32, 8, 128], P('dom', None, 'sub')
- coarse_residual: float32 [256, 32, 17], P('dom', 'sub')
The draws below stay inside these ranges and needn't reach their ends.
All inputs are finite; a program needn't handle non-finite values.
Results may differ from the reference program's by a relative error of at most 0.00008.
Values sent between devices are 32-bit elements; how exact they have to be, the bound alone decides.
A program may use at most 32 MiB of HBM per device.

```python
import math
import jax
import jax.numpy as jnp
import numpy as np
from jax import lax

GLL_PTS = 8
EZ = 16
NX = 256
NY = 32
N_DOM = 256


def level_of(key, shape, split, least, largest):
    factor_of, own = 1.0, jax.random.fold_in(key, 6)
    for dim, blocks in split:
        steps = jnp.exp(jax.random.uniform(jax.random.fold_in(own, dim), (blocks,), jnp.float32, least / len(split), largest / len(split)))
        factor_of = factor_of * jnp.repeat(steps, shape[dim] // blocks).reshape([-1 if axis == dim else 1 for axis in range(len(shape))])
    return factor_of


def scatter_about(key, dims, scale, bound, cuts=(), dtype=jnp.bfloat16):
    gain = level_of(key, dims, cuts, -0.22, 0.18) if cuts else 1.0
    entries = jax.random.normal(key, dims, jnp.float32) * scale * gain
    return jnp.minimum(jnp.maximum(entries, -bound), bound).astype(dtype)


def setup_inputs(seed: int = 0) -> dict:
    seeds = jax.random.split(jax.random.key(seed), 4)
    element_load = scatter_about(seeds[0], (NX, GLL_PTS, NY, GLL_PTS, GLL_PTS * EZ), 8.0, 48.0, ((0, 256), (2, 4)), jnp.float32)
    mobility = jnp.clip(jnp.exp(math.log(4.0) - 2.0794415 * jax.random.uniform(seeds[1], (NX, GLL_PTS, NY, GLL_PTS, GLL_PTS * EZ), jnp.float32) ** level_of(seeds[1], (NX, GLL_PTS, NY, GLL_PTS, GLL_PTS * EZ), ((0, 256), (2, 4)), -0.2, 0.2)), 0.5, 4.0)
    metric = jnp.clip(jnp.exp(math.log(2.0) - 1.3862944 * jax.random.uniform(seeds[2], (3, NX, NY, EZ), jnp.float32) ** level_of(seeds[2], (3, NX, NY, EZ), ((1, 256), (2, 4)), -0.2, 0.2)), 0.5, 2.0)
    return {"element_load": element_load, "mobility": mobility, "metric": metric}


GLL_NODES = np.array([-1.0, -0.8717401485096066, -0.5917001814331423, -0.2092992179024789, 0.2092992179024789, 0.5917001814331423, 0.8717401485096066, 1.0])
GLL_WEIGHTS = np.array([0.03571428571428571, 0.2107042271435061, 0.3411226924835044, 0.4124587946587038, 0.4124587946587038, 0.3411226924835044, 0.2107042271435061, 0.03571428571428571])
THETA = 1.65
DELTA = 1.35
RHO_FIRST = DELTA / THETA
RHO_SECOND = 1.0 / (2.0 * THETA / DELTA - RHO_FIRST)
EXACT = lax.Precision.HIGHEST


def derivative_table():
    identity = np.eye(8)
    differences = GLL_NODES[:, None] - GLL_NODES[None, :] + identity
    barycentric = 1.0 / np.prod(differences, axis=1)
    matrix = (barycentric[None, :] / barycentric[:, None]) / differences
    matrix = matrix * (1.0 - identity)
    row_sums = np.sum(matrix, axis=1)
    return matrix - identity * row_sums[:, None]


def make_tables():
    derivative = jnp.asarray(derivative_table(), jnp.float32)
    weights = jnp.asarray(GLL_WEIGHTS, jnp.float32)
    coarse_basis = jnp.asarray(np.stack([(1.0 - GLL_NODES) / 8.0, (1.0 + GLL_NODES) / 8.0], axis=1), jnp.float32)
    return derivative, weights, coarse_basis


def point_factors(mobility, metric, weights):
    spread = jnp.repeat(metric, 8, axis=3)[:, :, None, :, None, :]
    layers_z = mobility.shape[-1] // 8
    z_weights = jnp.tile(weights, layers_z)
    quadrature = weights[:, None, None, None] * weights[None, None, :, None] * z_weights
    return spread * (mobility * quadrature)


def apply_local(values, factors, derivative):
    full_shape = values.shape
    per_cell = values.reshape(full_shape[:4] + (full_shape[4] // 8, 8))
    grad_x = jnp.einsum('ai,xiyjc->xayjc', derivative, values, precision=EXACT)
    grad_y = jnp.einsum('bj,xiyjc->xiybc', derivative, values, precision=EXACT)
    grad_z = jnp.einsum('ck,xiyjek->xiyjec', derivative, per_cell, precision=EXACT).reshape(full_shape)
    flux_x = factors[0] * grad_x
    flux_y = factors[1] * grad_y
    flux_z = (factors[2] * grad_z).reshape(per_cell.shape)
    back_x = jnp.einsum('ai,xayjc->xiyjc', derivative, flux_x, precision=EXACT)
    back_y = jnp.einsum('bj,xiybc->xiyjc', derivative, flux_y, precision=EXACT)
    back_z = jnp.einsum('ck,xiyjec->xiyjek', derivative, flux_z, precision=EXACT).reshape(full_shape)
    return back_x + back_y + back_z


def diagonal_of(factors, derivative):
    squared = derivative * derivative
    full_shape = factors.shape[1:]
    per_cell = factors[2].reshape(full_shape[:4] + (full_shape[4] // 8, 8))
    part_x = jnp.einsum('ai,xayjc->xiyjc', squared, factors[0], precision=EXACT)
    part_y = jnp.einsum('bj,xiybc->xiyjc', squared, factors[1], precision=EXACT)
    part_z = jnp.einsum('ck,xiyjec->xiyjek', squared, per_cell, precision=EXACT).reshape(full_shape)
    return part_x + part_y + part_z


def split_blocks(array):
    return array.reshape((N_DOM, array.shape[0] // N_DOM) + array.shape[1:])


def metric_blocks(metric):
    return jnp.moveaxis(metric.reshape((3, N_DOM, metric.shape[1] // N_DOM) + metric.shape[2:]), 1, 0)


def operator_pass(values, mobility, metric):
    derivative, weights, coarse_basis = make_tables()

    def one_block(pieces):
        factors = point_factors(pieces[1], pieces[2], weights)
        return apply_local(pieces[0], factors, derivative)

    result = lax.map(one_block, (split_blocks(values), split_blocks(mobility), metric_blocks(metric)))
    return result.reshape(values.shape)


def assemble(values):
    upper = values[:, 7]
    bottom = values[:, 0]
    new_upper = upper + jnp.roll(bottom, -1, axis=0)
    new_bottom = bottom + jnp.roll(upper, 1, axis=0)
    values = jnp.concatenate([new_bottom[:, None], values[:, 1:7], new_upper[:, None]], axis=1)
    upper = values[:, :, :, 7]
    bottom = values[:, :, :, 0]
    new_upper = upper + jnp.roll(bottom, -1, axis=2)
    new_bottom = bottom + jnp.roll(upper, 1, axis=2)
    values = jnp.concatenate([new_bottom[:, :, :, None], values[:, :, :, 1:7], new_upper[:, :, :, None]], axis=3)
    full_shape = values.shape
    per_cell = values.reshape(full_shape[:4] + (full_shape[4] // 8, 8))
    upper = per_cell[..., 7]
    bottom = per_cell[..., 0]
    wall_pad = jnp.zeros_like(upper[..., :1])
    new_upper = upper + jnp.concatenate([bottom[..., 1:], wall_pad], axis=-1)
    new_bottom = bottom + jnp.concatenate([wall_pad, upper[..., :-1]], axis=-1)
    per_cell = jnp.concatenate([new_bottom[..., None], per_cell[..., 1:7], new_upper[..., None]], axis=-1)
    return per_cell.reshape(full_shape)


def coarse_pass(final_local, coarse_basis):
    full_shape = final_local.shape
    per_cell = final_local.reshape(full_shape[:4] + (full_shape[4] // 8, 8))
    along_z = jnp.einsum('ks,xiyjek->xiyjes', coarse_basis, per_cell, precision=EXACT)
    corners = jnp.einsum('ip,jq,xiyjes->xpyqes', coarse_basis, coarse_basis, along_z, precision=EXACT)
    edge_pad = jnp.zeros_like(corners[..., :1, 0])
    vertex_z = jnp.concatenate([corners[..., 0], edge_pad], axis=-1) + jnp.concatenate([edge_pad, corners[..., 1]], axis=-1)
    vertex_y = vertex_z[:, :, :, 0] + jnp.roll(vertex_z[:, :, :, 1], 1, axis=2)
    return vertex_y[:, 0] + jnp.roll(vertex_y[:, 1], 1, axis=0)


def reference(element_load, mobility, metric):
    derivative, weights, coarse_basis = make_tables()

    def diag_block(pieces):
        return diagonal_of(point_factors(pieces[0], pieces[1], weights), derivative)

    diag_local = lax.map(diag_block, (split_blocks(mobility), metric_blocks(metric))).reshape(mobility.shape)
    right_side = assemble(element_load)
    inverse = 1.0 / assemble(diag_local)
    first_step = inverse * right_side / THETA
    resid_first = right_side - assemble(operator_pass(first_step, mobility, metric))
    pressure = first_step + (RHO_SECOND * RHO_FIRST * first_step + (2.0 * RHO_SECOND / DELTA) * (inverse * resid_first))
    final_local = element_load - operator_pass(pressure, mobility, metric)
    return pressure, coarse_pass(final_local, coarse_basis)
```

```python
import jax
import jax.numpy as jnp
import numpy as np
from jax import lax
from jax.experimental import pallas as pl
from jax.experimental.pallas import tpu as pltpu
from jax.sharding import PartitionSpec as P

NODES = np.array(
    [
        -1.0,
        -0.8717401485096066,
        -0.5917001814331423,
        -0.2092992179024789,
        0.2092992179024789,
        0.5917001814331423,
        0.8717401485096066,
        1.0,
    ]
)
WEIGHTS = np.array(
    [
        0.03571428571428571,
        0.2107042271435061,
        0.3411226924835044,
        0.4124587946587038,
        0.4124587946587038,
        0.3411226924835044,
        0.2107042271435061,
        0.03571428571428571,
    ]
)
THETA = 1.65
DELTA = 1.35
RHO_FIRST = DELTA / THETA
RHO_SECOND = 1.0 / (2.0 * THETA / DELTA - RHO_FIRST)
KEEP = float(1.0 + RHO_SECOND * RHO_FIRST)
STEP = float(2.0 * RHO_SECOND / DELTA)
MESH = pl.DeviceIdType.MESH
F32 = jnp.float32
BF16 = jnp.bfloat16


def derivative_table():
    identity = np.eye(8)
    differences = NODES[:, None] - NODES[None, :] + identity
    barycentric = 1.0 / np.prod(differences, axis=1)
    matrix = barycentric[None, :] / barycentric[:, None] / differences
    matrix = matrix * (1.0 - identity)
    row_sums = np.sum(matrix, axis=1)
    return matrix - identity * row_sums[:, None]


DERIV = derivative_table()


def small_tables():
    deriv = DERIV.astype(np.float32).astype(np.float64)
    lower = (1.0 - NODES) / 8.0
    rows = [
        np.broadcast_to(np.tile(WEIGHTS, 16)[None, :], (8, 128)),
        np.tile(deriv.T, (1, 16)),
        np.tile(deriv, (1, 16)),
        np.tile(deriv * deriv, (1, 16)),
        np.broadcast_to(lower[:, None], (8, 128)),
    ]
    return np.stack(rows).astype(np.float32)


def total(terms):
    while len(terms) > 1:
        terms = [a + b for a, b in zip(terms[0::2], terms[1::2])] + (
            [terms[-1]] if len(terms) % 2 else []
        )
    return terms[0]


def apply_line(matrix, v, sign):
    even = [v[m] + v[7 - m] for m in range(4)]
    odd = [v[m] - v[7 - m] for m in range(4)]
    out = [None] * 8
    for a in range(4):
        with_even = total(
            [float((matrix[a, m] + matrix[a, 7 - m]) / 2) * even[m] for m in range(4)]
        )
        with_odd = total([float((matrix[a, m] - matrix[a, 7 - m]) / 2) * odd[m] for m in range(4)])
        out[a] = with_odd + with_even
        out[7 - a] = with_odd - with_even if sign < 0 else with_even - with_odd
    return out


def halves(x):
    high = x.astype(BF16)
    low = (x - high.astype(F32)).astype(BF16)
    return high, low


def wide_dot(x, table):
    high, low = halves(x)
    both = jnp.dot(jnp.concatenate([high, low], axis=1), table, preferred_element_type=F32)
    return both[:, :128] + both[:, 128:]


def kernel(
    load_hbm, mob_hbm, met_hbm, tab_hbm,
    press_hbm, coarse_ref,
    load_v, mob_v, met_v, tab_v, mats,
    fx, fy, fz, dg, rhs, fs, kv, zz, pr, out_v,
    sya, syb, sc,
    rxl, rxd, rya, rca, rxb, ryb, rcb, rc,
    local_sem, send_sem, recv_sem,
):
    d, s = lax.axis_index("dom"), lax.axis_index("sub")
    nd, ns = lax.axis_size("dom"), lax.axis_size("sub")
    dn, dp = lax.rem(d + 1, nd), lax.rem(d + nd - 1, nd)
    sn, sp = lax.rem(s + 1, ns), lax.rem(s + ns - 1, ns)

    fetch = [
        pltpu.make_async_copy(met_hbm, met_v, local_sem.at[0]),
        pltpu.make_async_copy(tab_hbm, tab_v, local_sem.at[1]),
        pltpu.make_async_copy(mob_hbm.at[0], mob_v, local_sem.at[2]),
        pltpu.make_async_copy(load_hbm.at[0], load_v, local_sem.at[3]),
    ]
    for copy in fetch:
        copy.start()
    barrier = pltpu.get_barrier_semaphore()
    around = [(a, b) for a in (dp, d, dn) for b in (sp, s, sn) if not (a is d and b is s)]
    for device in around:
        pl.semaphore_signal(barrier, inc=1, device_id=device, device_id_type=MESH)

    lane = lax.broadcasted_iota(jnp.int32, (8, 128), 1)
    sub8 = lax.broadcasted_iota(jnp.int32, (8, 128), 0)
    to_right = (lane % 8 == 7) & (lane != 127)
    to_left = (lane % 8 == 0) & (lane != 0)

    def z_joined(v):
        moved = jnp.where(to_right, pltpu.roll(v, 127, 1), pltpu.roll(v, 1, 1))
        return v + jnp.where(to_right | to_left, moved, 0.0)

    fetch[0].wait()
    fetch[1].wait()
    big_row = lax.broadcasted_iota(jnp.int32, (128, 128), 0)
    big_lane = lax.broadcasted_iota(jnp.int32, (128, 128), 1)
    same_cell = big_row // 8 == big_lane // 8

    def put_matrix(slot, matrix):
        high, low = halves(matrix)
        mats[slot, 0:128, 0:128] = high
        mats[slot, 0:128, 128:256] = low
        mats[slot, 128:256, 0:128] = high
        mats[slot, 128:256, 128:256] = jnp.zeros((128, 128), BF16)

    def tall(tile):
        return jnp.broadcast_to(tile[None], (16, 8, 128)).reshape(128, 128)

    for slot in range(3):
        put_matrix(slot, jnp.where(same_cell, tall(tab_v[1 + slot]), 0.0))
    lower = tall(tab_v[4])
    at_low, at_high = big_lane == big_row // 8, big_lane == big_row // 8 + 1
    put_matrix(3, jnp.where(at_low, lower, jnp.where(at_high, 0.25 - lower, 0.0)))
    put_matrix(4, jnp.where(at_low, -0.125, jnp.where(at_high, 0.125, 0.0)))

    cell_of = lax.broadcasted_iota(jnp.int32, (16, 128), 1) // 8
    expand = jnp.where(cell_of == lax.broadcasted_iota(jnp.int32, (16, 128), 0), 1.0, 0.0)
    spread = jnp.dot(
        met_v[...].reshape(24, 16), expand.astype(F32),
        preferred_element_type=F32, precision=lax.Precision.HIGHEST,
    ).reshape(3, 8, 128)
    base = [spread[n] * tab_v[0] for n in range(3)]

    fetch[2].wait()
    for i in range(8):
        for j in range(8):
            m = mob_v[i, :, j, :] * float(WEIGHTS[i] * WEIGHTS[j])
            fx[i, j] = m * base[0]
            fy[i, j] = m * base[1]
            fz[i, j] = m * base[2]
    zz[...] = wide_dot(fz[...].reshape(512, 128), mats[2]).reshape(8, 8, 8, 128)
    squared = DERIV * DERIV
    for j in range(8):
        line = apply_line(squared.T, [fx[i, j] for i in range(8)], 1)
        for i in range(8):
            dg[i, j] = line[i] + zz[i, j]
    for i in range(8):
        line = apply_line(squared.T, [fy[i, j] for j in range(8)], 1)
        for j in range(8):
            dg[i, j] = dg[i, j] + line[j]
    fetch[3].wait()
    sya[0, 0] = load_v[:, 7, 7, :]
    sya[1, 0] = load_v[:, 0, 0, :]
    sya[0, 1] = dg[:, 7, 7, :]
    sya[1, 1] = dg[:, 0, 0, :]

    used = [0]

    def send(src, dst, device):
        n = used[0]
        used[0] += 1
        copy = pltpu.make_async_remote_copy(
            src_ref=src, dst_ref=dst, send_sem=send_sem.at[n], recv_sem=recv_sem.at[n],
            device_id=device, device_id_type=MESH,
        )
        copy.start()
        return copy

    def send_lines(lines, corners, sides):
        return [
            send(lines.at[0], corners.at[0], (dn, sn)),
            send(lines.at[1], corners.at[1], (dn, sp)),
            send(lines.at[0], corners.at[2], (dp, sn)),
            send(lines.at[1], corners.at[3], (dp, sp)),
            send(lines.at[0], sides.at[0], (d, sn)),
            send(lines.at[1], sides.at[1], (d, sp)),
        ]

    pl.semaphore_wait(barrier, 8)
    first = send_lines(sya, rca, rya)
    first += [
        send(dg.at[7], rxd.at[0], (dn, s)),
        send(dg.at[0], rxd.at[1], (dp, s)),
        send(load_hbm.at[0, 7], rxl.at[0], (dn, s)),
        send(load_hbm.at[0, 0], rxl.at[1], (dp, s)),
    ]

    inner = range(1, 7)
    rim = [(i, j) for i in range(8) for j in range(8) if i in (0, 7) or j in (0, 7)]
    deep = [(i, j) for i in inner for j in inner]

    def first_step(i, j, load, diag):
        right = z_joined(load)
        inverse = 1.0 / z_joined(diag)
        rhs[i, j] = right
        dg[i, j] = inverse
        fs[i, j] = inverse * right * float(1.0 / THETA)

    def rim_sums(local, planes, sides, corners):
        out = {}
        rows = {}
        for i in range(8):
            line = {j: local(i, j) for j in (range(8) if i in (0, 7) else (0, 7))}
            if i == 0:
                line = {j: v + planes(0, j) for j, v in line.items()}
            if i == 7:
                line = {j: v + planes(1, j) for j, v in line.items()}
            before, after = sides(0, i), sides(1, i)
            if i == 0:
                before, after = before + corners(0, 7), after + corners(1, 7)
            if i == 7:
                before, after = before + corners(2, 0), after + corners(3, 0)
            low, high = line[0], line[7]
            line[7] = high + jnp.where(sub8 == 7, after, pltpu.roll(low, 7, 0))
            line[0] = low + jnp.where(sub8 == 0, before, pltpu.roll(high, 1, 0))
            for j, v in line.items():
                out[i, j] = v
        return out

    for i, j in deep:
        first_step(i, j, load_v[i, :, j, :], dg[i, j])

    for copy in first:
        copy.wait()
    wide = lambda row: jnp.broadcast_to(row, (8, 128))
    loads = rim_sums(
        lambda i, j: load_v[i, :, j, :],
        lambda side, j: rxl[side, :, j, :],
        lambda side, i: wide(rya[side, 0, i : i + 1, :]),
        lambda slot, i: wide(rca[slot, 0, i : i + 1, :]),
    )
    diags = rim_sums(
        lambda i, j: dg[i, j],
        lambda side, j: rxd[side, j],
        lambda side, i: wide(rya[side, 1, i : i + 1, :]),
        lambda slot, i: wide(rca[slot, 1, i : i + 1, :]),
    )
    for i, j in rim:
        first_step(i, j, loads[i, j], diags[i, j])

    flux = wide_dot(fs[...].reshape(512, 128), mats[0]) * fz[...].reshape(512, 128)
    zz[...] = wide_dot(flux, mats[1]).reshape(8, 8, 8, 128)
    for j in range(8):
        grad = apply_line(DERIV, [fs[i, j] for i in range(8)], -1)
        line = apply_line(DERIV.T, [fx[i, j] * grad[i] for i in range(8)], -1)
        for i in range(8):
            kv[i, j] = line[i] + zz[i, j]
    for i in range(8):
        grad = apply_line(DERIV, [fs[i, j] for j in range(8)], -1)
        line = apply_line(DERIV.T, [fy[i, j] * grad[j] for j in range(8)], -1)
        for j in range(8):
            kv[i, j] = kv[i, j] + line[j]
    syb[0] = kv[:, 7, 7, :]
    syb[1] = kv[:, 0, 0, :]
    second = send_lines(syb, rcb, ryb)
    second += [send(kv.at[7], rxb.at[0], (dn, s)), send(kv.at[0], rxb.at[1], (dp, s))]

    def smoothed(i, j, value):
        resid = rhs[i, j] - z_joined(value)
        p = KEEP * fs[i, j] + STEP * (dg[i, j] * resid)
        pr[i, j] = p
        out_v[i, :, j, :] = p

    for i, j in deep:
        smoothed(i, j, kv[i, j])
    for copy in second:
        copy.wait()
    sums = rim_sums(
        lambda i, j: kv[i, j],
        lambda side, j: rxb[side, j],
        lambda side, i: wide(ryb[side, i : i + 1, :]),
        lambda slot, i: wide(rcb[slot, i : i + 1, :]),
    )
    for i, j in rim:
        smoothed(i, j, sums[i, j])
    write = pltpu.make_async_copy(out_v, press_hbm.at[0], local_sem.at[0])
    write.start()

    def low_high(v):
        plain = total(v)
        slope = total([float(NODES[m]) * (v[m] - v[7 - m]) for m in range(4)])
        return (plain - slope) * 0.125, (plain + slope) * 0.125

    zz[...] = (
        wide_dot(pr[...].reshape(512, 128), mats[0]) * fz[...].reshape(512, 128)
    ).reshape(8, 8, 8, 128)
    along_x = []
    for j in range(8):
        grad = apply_line(DERIV, [pr[i, j] for i in range(8)], -1)
        along_x.append(total([fx[i, j] * grad[i] for i in range(8)]) * 0.125)
    along_y = []
    for i in range(8):
        grad = apply_line(DERIV, [pr[i, j] for j in range(8)], -1)
        along_y.append(total([fy[i, j] * grad[j] for j in range(8)]) * 0.125)
    x_part, y_part = low_high(along_x), low_high(along_y)
    held = [low_high([load_v[i, :, j, :] for i in range(8)]) for j in range(8)]
    flux_z = [low_high([zz[i, j] for i in range(8)]) for j in range(8)]
    plain, cells = [], []
    for p in range(2):
        held_p = low_high([held[j][p] for j in range(8)])
        flux_p = low_high([flux_z[j][p] for j in range(8)])
        for q in range(2):
            x_term = x_part[q] if p else -x_part[q]
            y_term = y_part[p] if q else -y_part[p]
            plain.append(held_p[q] - x_term - y_term)
            cells.append(-flux_p[q])
    vertex = wide_dot(jnp.concatenate(plain, axis=0), mats[3]) + wide_dot(
        jnp.concatenate(cells, axis=0), mats[4]
    )
    corner = [[vertex[16 * p + 8 * q : 16 * p + 8 * q + 8] for q in range(2)] for p in range(2)]
    row = []
    for p in range(2):
        moved = pltpu.roll(corner[p][1], 1, 0)
        row.append(corner[p][0] + jnp.where(sub8 == 0, 0.0, moved))
        sc[1 + p] = jnp.where(sub8 == 0, moved, 0.0)
    sc[0] = row[1]
    third = [
        send(sc.at[2], rc.at[2], (dn, sn)),
        send(sc.at[0], rc.at[0], (dn, s)),
        send(sc.at[1], rc.at[1], (d, sn)),
    ]
    for copy in third:
        copy.wait()
    coarse = row[0] + rc[0] + (rc[1] + rc[2])
    coarse_ref[0] = coarse[:, 0:17]
    write.wait()


def shards(element_load, mobility, metric):
    field = pltpu.VMEM((8, 8, 8, 128), F32)
    hbm = pl.BlockSpec(memory_space=pltpu.HBM)
    return pl.pallas_call(
        kernel,
        name="smoother",
        out_shape=(
            jax.ShapeDtypeStruct((1, 8, 8, 8, 128), F32),
            jax.ShapeDtypeStruct((1, 8, 17), F32),
        ),
        in_specs=[hbm, hbm, hbm, hbm],
        out_specs=(hbm, pl.BlockSpec(memory_space=pltpu.VMEM)),
        scratch_shapes=[
            field, field,
            pltpu.VMEM((3, 1, 8, 16), F32),
            pltpu.VMEM((5, 8, 128), F32),
            pltpu.VMEM((5, 256, 256), BF16),
            field, field, field, field, field, field, field, field, field, field,
            pltpu.VMEM((2, 2, 8, 128), F32),
            pltpu.VMEM((2, 8, 128), F32),
            pltpu.VMEM((3, 8, 128), F32),
            pltpu.VMEM((2, 8, 8, 128), F32),
            pltpu.VMEM((2, 8, 8, 128), F32),
            pltpu.VMEM((2, 2, 8, 128), F32),
            pltpu.VMEM((4, 2, 8, 128), F32),
            pltpu.VMEM((2, 8, 8, 128), F32),
            pltpu.VMEM((2, 8, 128), F32),
            pltpu.VMEM((4, 8, 128), F32),
            pltpu.VMEM((3, 8, 128), F32),
            pltpu.SemaphoreType.DMA((4,)),
            pltpu.SemaphoreType.DMA((21,)),
            pltpu.SemaphoreType.DMA((21,)),
        ],
        compiler_params=pltpu.CompilerParams(collective_id=0, has_side_effects=True),
    )(element_load, mobility, metric, jnp.asarray(small_tables()))


def solution(mesh):
    in_specs = (
        P("dom", None, "sub", None, None),
        P("dom", None, "sub", None, None),
        P(None, "dom", "sub", None),
    )
    out_specs = (P("dom", None, "sub", None, None), P("dom", "sub", None))
    return jax.shard_map(shards, mesh=mesh, in_specs=in_specs, out_specs=out_specs, check_vma=False)
```

```python
import jax
import jax.numpy as jnp
import numpy as np
from jax import lax
from jax.experimental import pallas as pl
from jax.experimental.pallas import tpu as pltpu
from jax.sharding import PartitionSpec as P

NODES = np.array(
    [
        -1.0,
        -0.8717401485096066,
        -0.5917001814331423,
        -0.2092992179024789,
        0.2092992179024789,
        0.5917001814331423,
        0.8717401485096066,
        1.0,
    ]
)
WEIGHTS = np.array(
    [
        0.03571428571428571,
        0.2107042271435061,
        0.3411226924835044,
        0.4124587946587038,
        0.4124587946587038,
        0.3411226924835044,
        0.2107042271435061,
        0.03571428571428571,
    ]
)
THETA = 1.65
DELTA = 1.35
RHO_FIRST = DELTA / THETA
RHO_SECOND = 1.0 / (2.0 * THETA / DELTA - RHO_FIRST)
KEEP = float(1.0 + RHO_SECOND * RHO_FIRST)
STEP = float(2.0 * RHO_SECOND / DELTA)
MESH = pl.DeviceIdType.MESH
F32 = jnp.float32
BF16 = jnp.bfloat16


def derivative_table():
    identity = np.eye(8)
    differences = NODES[:, None] - NODES[None, :] + identity
    barycentric = 1.0 / np.prod(differences, axis=1)
    matrix = barycentric[None, :] / barycentric[:, None] / differences
    matrix = matrix * (1.0 - identity)
    row_sums = np.sum(matrix, axis=1)
    return matrix - identity * row_sums[:, None]


DERIV = derivative_table()


def small_tables():
    deriv = DERIV.astype(np.float32).astype(np.float64)
    lower = (1.0 - NODES) / 8.0
    rows = [
        np.broadcast_to(np.tile(WEIGHTS, 16)[None, :], (8, 128)),
        np.tile(deriv.T, (1, 16)),
        np.tile(deriv, (1, 16)),
        np.tile(deriv * deriv, (1, 16)),
        np.broadcast_to(lower[:, None], (8, 128)),
    ]
    return np.stack(rows).astype(np.float32)


def total(terms):
    while len(terms) > 1:
        terms = [a + b for a, b in zip(terms[0::2], terms[1::2])] + (
            [terms[-1]] if len(terms) % 2 else []
        )
    return terms[0]


def apply_line(matrix, v, sign):
    even = [v[m] + v[7 - m] for m in range(4)]
    odd = [v[m] - v[7 - m] for m in range(4)]
    out = [None] * 8
    for a in range(4):
        with_even = total(
            [float((matrix[a, m] + matrix[a, 7 - m]) / 2) * even[m] for m in range(4)]
        )
        with_odd = total([float((matrix[a, m] - matrix[a, 7 - m]) / 2) * odd[m] for m in range(4)])
        out[a] = with_odd + with_even
        out[7 - a] = with_odd - with_even if sign < 0 else with_even - with_odd
    return out


def halves(x):
    high = x.astype(BF16)
    low = (x - high.astype(F32)).astype(BF16)
    return high, low


def wide_dot(x, table):
    high, low = halves(x)
    both = jnp.dot(jnp.concatenate([high, low], axis=1), table, preferred_element_type=F32)
    return both[:, :128] + both[:, 128:]


def kernel(
    load_hbm, mob_hbm, met_hbm, tab_hbm,
    press_ref, coarse_ref,
    load_v, mob_v, met_v, tab_v, mats,
    fx, fy, fz, dg, inv, rhs, fs, kv, zz, gx, gy, gz,
    hold, sya, sg, syb, sc,
    rxl, rxd, rxg, rya, rca, rxb, ryb, rcb, rc,
    local_sem, send_sem, recv_sem,
):
    d, s = lax.axis_index("dom"), lax.axis_index("sub")
    nd, ns = lax.axis_size("dom"), lax.axis_size("sub")
    dn, dp = lax.rem(d + 1, nd), lax.rem(d + nd - 1, nd)
    sn, sp = lax.rem(s + 1, ns), lax.rem(s + ns - 1, ns)

    fetch = [
        pltpu.make_async_copy(met_hbm, met_v, local_sem.at[0]),
        pltpu.make_async_copy(tab_hbm, tab_v, local_sem.at[1]),
        pltpu.make_async_copy(mob_hbm.at[0], mob_v, local_sem.at[2]),
        pltpu.make_async_copy(load_hbm.at[0], load_v, local_sem.at[3]),
    ]
    for copy in fetch:
        copy.start()
    barrier = pltpu.get_barrier_semaphore()
    around = [(a, b) for a in (dp, d, dn) for b in (sp, s, sn) if not (a is d and b is s)]
    for device in around:
        pl.semaphore_signal(barrier, inc=1, device_id=device, device_id_type=MESH)

    lane = lax.broadcasted_iota(jnp.int32, (8, 128), 1)
    sub8 = lax.broadcasted_iota(jnp.int32, (8, 128), 0)
    to_right = (lane % 8 == 7) & (lane != 127)
    to_left = (lane % 8 == 0) & (lane != 0)

    def z_joined(v):
        moved = jnp.where(to_right, pltpu.roll(v, 127, 1), pltpu.roll(v, 1, 1))
        return v + jnp.where(to_right | to_left, moved, 0.0)

    fetch[0].wait()
    fetch[1].wait()
    big_row = lax.broadcasted_iota(jnp.int32, (128, 128), 0)
    big_lane = lax.broadcasted_iota(jnp.int32, (128, 128), 1)
    same_cell = big_row // 8 == big_lane // 8

    def put_matrix(slot, matrix):
        high, low = halves(matrix)
        mats[slot, 0:128, 0:128] = high
        mats[slot, 0:128, 128:256] = low
        mats[slot, 128:256, 0:128] = high
        mats[slot, 128:256, 128:256] = jnp.zeros((128, 128), BF16)

    def tall(tile):
        return jnp.broadcast_to(tile[None], (16, 8, 128)).reshape(128, 128)

    for slot in range(3):
        put_matrix(slot, jnp.where(same_cell, tall(tab_v[1 + slot]), 0.0))
    lower = tall(tab_v[4])
    at_low, at_high = big_lane == big_row // 8, big_lane == big_row // 8 + 1
    put_matrix(3, jnp.where(at_low, lower, jnp.where(at_high, 0.25 - lower, 0.0)))
    put_matrix(4, jnp.where(at_low, -0.125, jnp.where(at_high, 0.125, 0.0)))

    cell_of = lax.broadcasted_iota(jnp.int32, (16, 128), 1) // 8
    expand = jnp.where(cell_of == lax.broadcasted_iota(jnp.int32, (16, 128), 0), 1.0, 0.0)
    spread = jnp.dot(
        met_v[...].reshape(24, 16), expand.astype(F32),
        preferred_element_type=F32, precision=lax.Precision.HIGHEST,
    ).reshape(3, 8, 128)
    base = [spread[n] * tab_v[0] for n in range(3)]

    fetch[2].wait()
    for i in range(8):
        for j in range(8):
            m = mob_v[i, :, j, :] * float(WEIGHTS[i] * WEIGHTS[j])
            fx[i, j] = m * base[0]
            fy[i, j] = m * base[1]
            fz[i, j] = m * base[2]
    zz[...] = wide_dot(fz[...].reshape(512, 128), mats[2]).reshape(8, 8, 8, 128)
    squared = DERIV * DERIV
    for j in range(8):
        line = apply_line(squared.T, [fx[i, j] for i in range(8)], 1)
        for i in range(8):
            dg[i, j] = line[i] + zz[i, j]
    for i in range(8):
        line = apply_line(squared.T, [fy[i, j] for j in range(8)], 1)
        for j in range(8):
            dg[i, j] = dg[i, j] + line[j]
    fetch[3].wait()
    sya[0, 0] = load_v[:, 7, 7, :]
    sya[1, 0] = load_v[:, 0, 0, :]
    sya[0, 1] = dg[:, 7, 7, :]
    sya[1, 1] = dg[:, 0, 0, :]

    used = [0]

    def send(src, dst, device):
        n = used[0]
        used[0] += 1
        copy = pltpu.make_async_remote_copy(
            src_ref=src, dst_ref=dst, send_sem=send_sem.at[n], recv_sem=recv_sem.at[n],
            device_id=device, device_id_type=MESH,
        )
        copy.start()
        return copy

    def send_lines(lines, corners, sides):
        return [
            send(lines.at[0], corners.at[0], (dn, sn)),
            send(lines.at[1], corners.at[1], (dn, sp)),
            send(lines.at[0], corners.at[2], (dp, sn)),
            send(lines.at[1], corners.at[3], (dp, sp)),
            send(lines.at[0], sides.at[0], (d, sn)),
            send(lines.at[1], sides.at[1], (d, sp)),
        ]

    pl.semaphore_wait(barrier, 8)
    first = send_lines(sya, rca, rya)
    first += [
        send(dg.at[7], rxd.at[0], (dn, s)),
        send(dg.at[0], rxd.at[1], (dp, s)),
        send(load_hbm.at[0, 7], rxl.at[0], (dn, s)),
        send(load_hbm.at[0, 0], rxl.at[1], (dp, s)),
    ]

    inner = range(1, 7)
    rim = [(i, j) for i in range(8) for j in range(8) if i in (0, 7) or j in (0, 7)]
    deep = [(i, j) for i in inner for j in inner]

    def first_step(i, j, load, diag):
        right = z_joined(load)
        inverse = 1.0 / z_joined(diag)
        rhs[i, j] = right
        inv[i, j] = inverse
        fs[i, j] = inverse * right * float(1.0 / THETA)

    def rim_sums(planes_i, local, planes, sides, corners):
        out = {}
        for i in planes_i:
            line = {j: local(i, j) for j in (range(8) if i in (0, 7) else (0, 7))}
            before, after = sides(0, i), sides(1, i)
            if i == 0:
                line = {j: v + planes(0, j) for j, v in line.items()}
                before, after = before + corners(0, 7), after + corners(1, 7)
            if i == 7:
                line = {j: v + planes(1, j) for j, v in line.items()}
                before, after = before + corners(2, 0), after + corners(3, 0)
            low, high = line[0], line[7]
            line[7] = high + jnp.where(sub8 == 7, after, pltpu.roll(low, 7, 0))
            line[0] = low + jnp.where(sub8 == 0, before, pltpu.roll(high, 1, 0))
            for j, v in line.items():
                out[i, j] = v
        return out

    gz[...] = wide_dot(fz[...].reshape(512, 128), mats[1]).reshape(8, 8, 8, 128)
    for j in range(8):
        line = apply_line(DERIV.T / 8.0, [fx[i, j] for i in range(8)], -1)
        for i in range(8):
            gx[i, j] = line[i]
        sg[0, j] = line[7]
    for i in range(8):
        line = apply_line(DERIV.T / 8.0, [fy[i, j] for j in range(8)], -1)
        for j in range(8):
            gy[i, j] = line[j]
            if i == 7:
                sg[1, j] = line[j]
    for j in range(8):
        sg[2, j] = gz[7, j]
    first.append(send(sg, rxg, (dn, s)))

    for i, j in deep:
        first_step(i, j, load_v[i, :, j, :], dg[i, j])

    def low_high(v):
        plain = total(v)
        slope = total([float(NODES[m]) * (v[m] - v[7 - m]) for m in range(4)])
        return (plain - slope) * 0.125, (plain + slope) * 0.125

    held = [low_high([load_v[i, :, j, :] for i in range(8)]) for j in range(8)]
    held = [low_high([held[j][p] for j in range(8)]) for p in range(2)]
    for p in range(2):
        for q in range(2):
            hold[2 * p + q] = held[p][q]

    for copy in first[:10]:
        copy.wait_recv()
    wide = lambda row: jnp.broadcast_to(row, (8, 128))
    loads = rim_sums(
        range(8),
        lambda i, j: load_v[i, :, j, :],
        lambda side, j: rxl[side, :, j, :],
        lambda side, i: wide(rya[side, 0, i : i + 1, :]),
        lambda slot, i: wide(rca[slot, 0, i : i + 1, :]),
    )
    diags = rim_sums(
        range(8),
        lambda i, j: dg[i, j],
        lambda side, j: rxd[side, j],
        lambda side, i: wide(rya[side, 1, i : i + 1, :]),
        lambda slot, i: wide(rca[slot, 1, i : i + 1, :]),
    )
    for i, j in rim:
        first_step(i, j, loads[i, j], diags[i, j])

    flux = wide_dot(fs[...].reshape(512, 128), mats[0]) * fz[...].reshape(512, 128)
    zz[...] = wide_dot(flux, mats[1]).reshape(8, 8, 8, 128)
    for j in range(8):
        grad = apply_line(DERIV, [fs[i, j] for i in range(8)], -1)
        line = apply_line(DERIV.T, [fx[i, j] * grad[i] for i in range(8)], -1)
        for i in range(8):
            kv[i, j] = line[i] + zz[i, j]
    for i in range(8):
        grad = apply_line(DERIV, [fs[i, j] for j in range(8)], -1)
        line = apply_line(DERIV.T, [fy[i, j] * grad[j] for j in range(8)], -1)
        for j in range(8):
            kv[i, j] = kv[i, j] + line[j]
    syb[0] = kv[:, 7, 7, :]
    syb[1] = kv[:, 0, 0, :]
    second = send_lines(syb, rcb, ryb)
    second += [send(kv.at[7], rxb.at[0], (dn, s)), send(kv.at[0], rxb.at[1], (dp, s))]

    weight = [[float((1.0 + (2 * p - 1) * NODES[m]) / 8.0) for m in range(8)] for p in range(2)]
    part_x, part_y, part_z = [[] for _ in range(8)], [[] for _ in range(8)], {}

    def smoothed(i, j, value):
        resid = rhs[i, j] - z_joined(value)
        p = KEEP * fs[i, j] + STEP * (inv[i, j] * resid)
        fs[i, j] = p
        press_ref[0, i, :, j, :] = p

    for i, j in deep:
        smoothed(i, j, kv[i, j])

    def finish(planes_i):
        sums = rim_sums(
            planes_i,
            lambda i, j: kv[i, j],
            lambda side, j: rxb[side, j],
            lambda side, i: wide(ryb[side, i : i + 1, :]),
            lambda slot, i: wide(rcb[slot, i : i + 1, :]),
        )
        for (i, j), value in sums.items():
            smoothed(i, j, value)

    def weigh(line, p):
        return total([weight[p][m] * v for m, v in enumerate(line) if weight[p][m] != 0.0])

    def vertices(plain, cells):
        both = wide_dot(jnp.concatenate(plain, axis=0), mats[3]) + wide_dot(
            jnp.concatenate(cells, axis=0), mats[4]
        )
        inside, edge = both[0:8], pltpu.roll(both[8:16], 1, 0)
        return inside + jnp.where(sub8 == 0, 0.0, edge), jnp.where(sub8 == 0, edge, 0.0)

    for n in (4, 5):
        second[n].wait_recv()
    finish(inner)
    for n in (0, 1, 6):
        second[n].wait_recv()
    finish((0,))
    x_sum = [total([gx[i, j] * fs[i, j] for i in range(7)]) for j in range(8)]
    y_sum = [total([gy[i, j] * fs[i, j] for j in range(8)]) for i in range(7)]
    z_line = []
    for i in range(7):
        terms = [gz[i, j] * fs[i, j] for j in range(8)]
        z_line.append([weigh(terms, q) for q in range(2)])
    y_high = weigh(y_sum, 1)
    plain = [
        hold[2] - weigh(x_sum, 0) + y_high,
        hold[3] - weigh(x_sum, 1) - y_high,
    ]
    cells = [-weigh([z[q] for z in z_line], 1) for q in range(2)]
    sc[0], sc[1] = vertices(plain, cells)
    third = [
        send(sc.at[1], rc.at[1], (dn, sn)),
        send(sc.at[0], rc.at[0], (dn, s)),
    ]
    for n in (2, 3, 7):
        second[n].wait_recv()
    finish((7,))
    first[10].wait_recv()
    x_sum = [x_sum[j] + gx[7, j] * fs[7, j] for j in range(8)]
    y_low = weigh(y_sum + [y_sum[0]], 0)
    x_net = [x_sum[j] - rxg[0, j] * fs[0, j] for j in range(8)]
    y_face = 0.25 * total([rxg[1, j] * fs[0, j] for j in range(8)])
    z_face = [rxg[2, j] * fs[0, j] for j in range(8)]
    plain = [
        hold[0] + weigh(x_net, 0) + (y_low + y_face),
        hold[1] + weigh(x_net, 1) - (y_low + y_face),
    ]
    cells = [
        -weigh([z[q] for z in z_line] + [z_line[0][q]], 0) - 0.25 * weigh(z_face, q)
        for q in range(2)
    ]
    own, sc[2] = vertices(plain, cells)
    third.append(send(sc.at[2], rc.at[2], (d, sn)))
    for copy in third:
        copy.wait_recv()
    coarse = own + rc[0] + (rc[1] + rc[2])
    coarse_ref[0] = coarse[:, 0:17]
    for copy in first + second + third:
        copy.wait_send()


def shards(element_load, mobility, metric):
    field = pltpu.VMEM((8, 8, 8, 128), F32)
    hbm = pl.BlockSpec(memory_space=pltpu.HBM)
    vmem = pl.BlockSpec(memory_space=pltpu.VMEM)
    return pl.pallas_call(
        kernel,
        name="smoother",
        out_shape=(
            pltpu.VMEM((1, 8, 8, 8, 128), F32),
            pltpu.VMEM((1, 8, 17), F32),
        ),
        in_specs=[hbm, hbm, hbm, hbm],
        out_specs=(vmem, vmem),
        scratch_shapes=[
            field, field,
            pltpu.VMEM((3, 1, 8, 16), F32),
            pltpu.VMEM((5, 8, 128), F32),
            pltpu.VMEM((5, 256, 256), BF16),
            *[field] * 12,
            pltpu.VMEM((4, 8, 128), F32),
            pltpu.VMEM((2, 2, 8, 128), F32),
            pltpu.VMEM((3, 8, 8, 128), F32),
            pltpu.VMEM((2, 8, 128), F32),
            pltpu.VMEM((3, 8, 128), F32),
            pltpu.VMEM((2, 8, 8, 128), F32),
            pltpu.VMEM((2, 8, 8, 128), F32),
            pltpu.VMEM((3, 8, 8, 128), F32),
            pltpu.VMEM((2, 2, 8, 128), F32),
            pltpu.VMEM((4, 2, 8, 128), F32),
            pltpu.VMEM((2, 8, 8, 128), F32),
            pltpu.VMEM((2, 8, 128), F32),
            pltpu.VMEM((4, 8, 128), F32),
            pltpu.VMEM((3, 8, 128), F32),
            pltpu.SemaphoreType.DMA((4,)),
            pltpu.SemaphoreType.DMA((22,)),
            pltpu.SemaphoreType.DMA((22,)),
        ],
        compiler_params=pltpu.CompilerParams(collective_id=0, has_side_effects=True),
    )(element_load, mobility, metric, jnp.asarray(small_tables()))


def solution(mesh):
    in_specs = (
        P("dom", None, "sub", None, None),
        P("dom", None, "sub", None, None),
        P(None, "dom", "sub", None),
    )
    out_specs = (P("dom", None, "sub", None, None), P("dom", "sub", None))
    return jax.shard_map(shards, mesh=mesh, in_specs=in_specs, out_specs=out_specs, check_vma=False)
```

```python
import jax
import jax.numpy as jnp
import numpy as np
from jax import lax
from jax.experimental import pallas as pl
from jax.experimental.pallas import tpu as pltpu
from jax.sharding import PartitionSpec as P

NODES = np.array(
    [
        -1.0,
        -0.8717401485096066,
        -0.5917001814331423,
        -0.2092992179024789,
        0.2092992179024789,
        0.5917001814331423,
        0.8717401485096066,
        1.0,
    ]
)
WEIGHTS = np.array(
    [
        0.03571428571428571,
        0.2107042271435061,
        0.3411226924835044,
        0.4124587946587038,
        0.4124587946587038,
        0.3411226924835044,
        0.2107042271435061,
        0.03571428571428571,
    ]
)
THETA = 1.65
DELTA = 1.35
RHO_FIRST = DELTA / THETA
RHO_SECOND = 1.0 / (2.0 * THETA / DELTA - RHO_FIRST)
KEEP = float(1.0 + RHO_SECOND * RHO_FIRST)
STEP = float(2.0 * RHO_SECOND / DELTA)
MESH = pl.DeviceIdType.MESH
F32 = jnp.float32
BF16 = jnp.bfloat16


def derivative_table():
    identity = np.eye(8)
    differences = NODES[:, None] - NODES[None, :] + identity
    barycentric = 1.0 / np.prod(differences, axis=1)
    matrix = barycentric[None, :] / barycentric[:, None] / differences
    matrix = matrix * (1.0 - identity)
    row_sums = np.sum(matrix, axis=1)
    return matrix - identity * row_sums[:, None]


DERIV = derivative_table()


def small_tables():
    deriv = DERIV.astype(np.float32).astype(np.float64)
    lower = (1.0 - NODES) / 8.0
    rows = [
        np.broadcast_to(np.tile(WEIGHTS, 16)[None, :], (8, 128)),
        np.tile(deriv.T, (1, 16)),
        np.tile(deriv, (1, 16)),
        np.tile(deriv * deriv, (1, 16)),
        np.broadcast_to(lower[:, None], (8, 128)),
    ]
    return np.stack(rows).astype(np.float32)


def total(terms):
    while len(terms) > 1:
        terms = [a + b for a, b in zip(terms[0::2], terms[1::2])] + (
            [terms[-1]] if len(terms) % 2 else []
        )
    return terms[0]


def apply_line(matrix, v, sign):
    pair = [(v[m], v[7 - m]) for m in range(4)]
    even = [x if y is None else x + y for x, y in pair]
    odd = [x if y is None else x - y for x, y in pair]
    out = [None] * 8
    for a in range(4):
        with_even = total(
            [float((matrix[a, m] + matrix[a, 7 - m]) / 2) * even[m] for m in range(4)]
        )
        with_odd = total([float((matrix[a, m] - matrix[a, 7 - m]) / 2) * odd[m] for m in range(4)])
        out[a] = with_odd + with_even
        out[7 - a] = with_odd - with_even if sign < 0 else with_even - with_odd
    return out


def halves(x):
    high = x.astype(BF16)
    low = (x - high.astype(F32)).astype(BF16)
    return high, low


def wide_dot(x, table):
    high, low = halves(x)
    both = jnp.dot(jnp.concatenate([high, low], axis=1), table, preferred_element_type=F32)
    return both[:, :128] + both[:, 128:]


def kernel(
    load_hbm, mob_hbm, met_hbm, tab_hbm,
    press_ref, coarse_ref,
    load_v, mob_v, met_v, tab_v, mats,
    fx, fy, fz, dg, inv, rhs, fs, kv, zz, gx, gy, gz, k7,
    hold, sya, sg, sgx, sk, syb, sye, syc, sc,
    rxl, rxd, rxg, rxgx, rya, rca, rk, rxb, ryb, rcb, rc,
    local_sem, send_sem, recv_sem,
):
    d, s = lax.axis_index("dom"), lax.axis_index("sub")
    nd, ns = lax.axis_size("dom"), lax.axis_size("sub")
    dn, dp = lax.rem(d + 1, nd), lax.rem(d + nd - 1, nd)
    sn, sp = lax.rem(s + 1, ns), lax.rem(s + ns - 1, ns)

    fetch = [
        pltpu.make_async_copy(met_hbm, met_v, local_sem.at[0]),
        pltpu.make_async_copy(tab_hbm, tab_v, local_sem.at[1]),
        pltpu.make_async_copy(mob_hbm.at[0], mob_v, local_sem.at[2]),
        pltpu.make_async_copy(load_hbm.at[0], load_v, local_sem.at[3]),
    ]
    for copy in fetch:
        copy.start()
    barrier = pltpu.get_barrier_semaphore()
    around = [(a, b) for a in (dp, d, dn) for b in (sp, s, sn) if not (a is d and b is s)]
    for device in around:
        pl.semaphore_signal(barrier, inc=1, device_id=device, device_id_type=MESH)

    lane = lax.broadcasted_iota(jnp.int32, (8, 128), 1)
    sub8 = lax.broadcasted_iota(jnp.int32, (8, 128), 0)
    to_right = (lane % 8 == 7) & (lane != 127)
    to_left = (lane % 8 == 0) & (lane != 0)

    def z_joined(v):
        moved = jnp.where(to_right, pltpu.roll(v, 127, 1), pltpu.roll(v, 1, 1))
        return v + jnp.where(to_right | to_left, moved, 0.0)

    fetch[0].wait()
    fetch[1].wait()
    big_row = lax.broadcasted_iota(jnp.int32, (128, 128), 0)
    big_lane = lax.broadcasted_iota(jnp.int32, (128, 128), 1)
    same_cell = big_row // 8 == big_lane // 8

    def put_matrix(slot, matrix):
        high, low = halves(matrix)
        mats[slot, 0:128, 0:128] = high
        mats[slot, 0:128, 128:256] = low
        mats[slot, 128:256, 0:128] = high
        mats[slot, 128:256, 128:256] = jnp.zeros((128, 128), BF16)

    def tall(tile):
        return jnp.broadcast_to(tile[None], (16, 8, 128)).reshape(128, 128)

    for slot in range(3):
        put_matrix(slot, jnp.where(same_cell, tall(tab_v[1 + slot]), 0.0))
    lower = tall(tab_v[4])
    at_low, at_high = big_lane == big_row // 8, big_lane == big_row // 8 + 1
    put_matrix(3, jnp.where(at_low, lower, jnp.where(at_high, 0.25 - lower, 0.0)))
    put_matrix(4, jnp.where(at_low, -0.125, jnp.where(at_high, 0.125, 0.0)))

    cell_of = lax.broadcasted_iota(jnp.int32, (16, 128), 1) // 8
    expand = jnp.where(cell_of == lax.broadcasted_iota(jnp.int32, (16, 128), 0), 1.0, 0.0)
    spread = jnp.dot(
        met_v[...].reshape(24, 16), expand.astype(F32),
        preferred_element_type=F32, precision=lax.Precision.HIGHEST,
    ).reshape(3, 8, 128)
    base = [spread[n] * tab_v[0] for n in range(3)]

    fetch[2].wait()
    for i in range(8):
        for j in range(8):
            m = mob_v[i, :, j, :] * float(WEIGHTS[i] * WEIGHTS[j])
            fx[i, j] = m * base[0]
            fy[i, j] = m * base[1]
            fz[i, j] = m * base[2]
            if i == 7:
                sg[j] = m
    sg[8] = base[1]
    sg[9] = base[2]
    zz[...] = wide_dot(fz[...].reshape(512, 128), mats[2]).reshape(8, 8, 8, 128)
    squared = DERIV * DERIV
    for j in range(8):
        line = apply_line(squared.T, [fx[i, j] for i in range(8)], 1)
        for i in range(8):
            dg[i, j] = line[i] + zz[i, j]
        sg[10 + j] = line[7]
    for i in range(8):
        line = apply_line(squared.T, [fy[i, j] for j in range(8)], 1)
        for j in range(8):
            dg[i, j] = dg[i, j] + line[j]
    fetch[3].wait()
    sya[0, 0] = load_v[:, 7, 7, :]
    sya[1, 0] = load_v[:, 0, 0, :]
    sya[0, 1] = dg[:, 7, 7, :]
    sya[1, 1] = dg[:, 0, 0, :]

    used = [0]

    def send(src, dst, device):
        n = used[0]
        used[0] += 1
        copy = pltpu.make_async_remote_copy(
            src_ref=src, dst_ref=dst, send_sem=send_sem.at[n], recv_sem=recv_sem.at[n],
            device_id=device, device_id_type=MESH,
        )
        copy.start()
        return copy

    pl.semaphore_wait(barrier, 8)
    first = [
        send(sya.at[0], rca.at[0], (dn, sn)),
        send(sya.at[1], rca.at[1], (dn, sp)),
        send(sya.at[0], rca.at[2], (dp, sn)),
        send(sya.at[1], rca.at[3], (dp, sp)),
        send(sya.at[0], rya.at[0], (d, sn)),
        send(sya.at[1], rya.at[1], (d, sp)),
        send(dg.at[7], rxd.at[0], (dn, s)),
        send(dg.at[0], rxd.at[1], (dp, s)),
        send(load_hbm.at[0, 7], rxl.at[0], (dn, s)),
        send(load_hbm.at[0, 0], rxl.at[1], (dp, s)),
        send(sg, rxg, (dn, s)),
    ]

    inner = range(1, 7)
    rim = [(i, j) for i in range(8) for j in range(8) if i in (0, 7) or j in (0, 7)]
    deep = [(i, j) for i in inner for j in inner]

    def first_step(i, j, load, diag):
        right = z_joined(load)
        inverse = 1.0 / z_joined(diag)
        rhs[i, j] = right
        inv[i, j] = inverse
        fs[i, j] = inverse * right * float(1.0 / THETA)

    def rim_sums(planes_i, local, planes, sides, corners):
        out = {}
        for i in planes_i:
            line = {j: local(i, j) for j in (range(8) if i in (0, 7) else (0, 7))}
            before, after = sides(0, i), sides(1, i)
            if i == 0:
                line = {j: v + planes(0, j) for j, v in line.items()}
                before, after = before + corners(0, 7), after + corners(1, 7)
            if i == 7:
                line = {j: v + planes(1, j) for j, v in line.items()}
                before, after = before + corners(2, 0), after + corners(3, 0)
            low, high = line[0], line[7]
            line[7] = high + jnp.where(sub8 == 7, after, pltpu.roll(low, 7, 0))
            line[0] = low + jnp.where(sub8 == 0, before, pltpu.roll(high, 1, 0))
            for j, v in line.items():
                out[i, j] = v
        return out

    for j in range(8):
        line = [fx[a, j] for a in range(8)]
        for i in range(7):
            k7[i, j] = total([float(DERIV[a, i] * DERIV[a, 7]) * line[a] for a in range(8)])
        line = apply_line(DERIV.T / 8.0, line, -1)
        for i in range(8):
            gx[i, j] = line[i]
        sgx[j] = line[7]
        k7[7, j] = jnp.zeros((8, 128), F32)
    sk[0] = k7[:, 7, 7, :]
    sk[1] = k7[:, 0, 0, :]
    first += [
        send(sk.at[0], rk.at[0], (d, sn)),
        send(sk.at[1], rk.at[1], (d, sp)),
        send(sgx, rxgx, (dn, s)),
    ]
    gz[1:7] = wide_dot(fz[1:7].reshape(384, 128), mats[1]).reshape(6, 8, 8, 128)
    for i in range(1, 7):
        line = apply_line(DERIV.T / 8.0, [fy[i, j] for j in range(8)], -1)
        for j in range(8):
            gy[i, j] = line[j]

    for i, j in deep:
        first_step(i, j, load_v[i, :, j, :], dg[i, j])

    def low_high(v):
        plain = total(v)
        slope = total([float(NODES[m]) * (v[m] - v[7 - m]) for m in range(4)])
        return (plain - slope) * 0.125, (plain + slope) * 0.125

    held = [low_high([load_v[i, :, j, :] for i in range(8)]) for j in range(8)]
    held = [low_high([held[j][p] for j in range(8)]) for p in range(2)]
    for p in range(2):
        for q in range(2):
            hold[2 * p + q] = held[p][q]

    wide = lambda row: jnp.broadcast_to(row, (8, 128))

    def start_rim(planes_i):
        loads = rim_sums(
            planes_i,
            lambda i, j: load_v[i, :, j, :],
            lambda side, j: rxl[side, :, j, :],
            lambda side, i: wide(rya[side, 0, i : i + 1, :]),
            lambda slot, i: wide(rca[slot, 0, i : i + 1, :]),
        )
        diags = rim_sums(
            planes_i,
            lambda i, j: dg[i, j],
            lambda side, j: rxd[side, j],
            lambda side, i: wide(rya[side, 1, i : i + 1, :]),
            lambda slot, i: wide(rca[slot, 1, i : i + 1, :]),
        )
        for i, j in loads:
            first_step(i, j, loads[i, j], diags[i, j])

    for n in (4, 5):
        first[n].wait_recv()
    start_rim(inner)
    for n in (0, 1, 6, 8):
        first[n].wait_recv()
    start_rim((0,))
    for j in range(8):
        grad = apply_line(DERIV, [fs[i, j] for i in range(7)] + [None], -1)
        line = apply_line(DERIV.T, [fx[i, j] * grad[i] for i in range(8)], -1)
        for i in range(8):
            kv[i, j] = line[i]
    sye[0] = kv[:, 7, 7, :]
    sye[1] = kv[:, 0, 0, :]
    second = [
        send(sye.at[0], rcb.at[0], (dn, sn)),
        send(sye.at[1], rcb.at[1], (dn, sp)),
        send(kv.at[7], rxb.at[0], (dn, s)),
    ]

    def yz_part(low, high):
        rows = 64 * (high - low)
        flux = wide_dot(fs[low:high].reshape(rows, 128), mats[0]) * fz[low:high].reshape(rows, 128)
        zz[low:high] = wide_dot(flux, mats[1]).reshape(high - low, 8, 8, 128)
        for i in range(low, high):
            grad = apply_line(DERIV, [fs[i, j] for j in range(8)], -1)
            line = apply_line(DERIV.T, [fy[i, j] * grad[j] for j in range(8)], -1)
            for j in range(8):
                kv[i, j] = kv[i, j] + (line[j] + zz[i, j])

    yz_part(1, 7)
    first[10].wait_recv()
    for j in range(8):
        fy[0, j] = fy[0, j] + rxg[j] * rxg[8]
        fz[0, j] = fz[0, j] + rxg[j] * rxg[9]
        kv[0, j] = kv[0, j] + rxg[10 + j] * fs[0, j]
    yz_part(0, 1)
    syb[0] = kv[:, 7, 7, :]
    syb[1] = kv[:, 0, 0, :]
    second += [send(syb.at[0], ryb.at[0], (d, sn)), send(syb.at[1], ryb.at[1], (d, sp))]

    for n in (2, 3, 7, 9):
        first[n].wait_recv()
    start_rim((7,))
    for j in range(8):
        v = fs[7, j]
        for i in range(7):
            kv[i, j] = kv[i, j] + k7[i, j] * v
    syc[0] = kv[:, 7, 7, :]
    syc[1] = kv[:, 0, 0, :]
    second += [
        send(syc.at[0], rcb.at[2], (dp, sn)),
        send(syc.at[1], rcb.at[3], (dp, sp)),
        send(kv.at[0], rxb.at[1], (dp, s)),
    ]
    gz[0] = wide_dot(fz[0].reshape(64, 128), mats[1]).reshape(8, 8, 128)
    line = apply_line(DERIV.T / 8.0, [fy[0, j] for j in range(8)], -1)
    for j in range(8):
        gy[0, j] = line[j]
    for n in (11, 12):
        first[n].wait_recv()
    ends = [fs[7, 0], fs[7, 7]]

    weight = [[float((1.0 + (2 * p - 1) * NODES[m]) / 8.0) for m in range(8)] for p in range(2)]
    part_x, part_y, part_z = [[] for _ in range(8)], [[] for _ in range(8)], {}

    def smoothed(i, j, value):
        resid = rhs[i, j] - z_joined(value)
        p = KEEP * fs[i, j] + STEP * (inv[i, j] * resid)
        fs[i, j] = p
        press_ref[0, i, :, j, :] = p

    for i, j in deep:
        smoothed(i, j, kv[i, j])

    def finish(planes_i):
        sums = rim_sums(
            planes_i,
            lambda i, j: kv[i, j],
            lambda side, j: rxb[side, j],
            lambda side, i: wide(ryb[side, i : i + 1, :])
            + (wide(rk[side, i : i + 1, :]) * ends[side] if i < 7 else 0.0),
            lambda slot, i: wide(rcb[slot, i : i + 1, :]),
        )
        for (i, j), value in sums.items():
            smoothed(i, j, value)

    def weigh(line, p):
        return total([weight[p][m] * v for m, v in enumerate(line) if weight[p][m] != 0.0])

    def vertices(plain, cells):
        both = wide_dot(jnp.concatenate(plain, axis=0), mats[3]) + wide_dot(
            jnp.concatenate(cells, axis=0), mats[4]
        )
        inside, edge = both[0:8], pltpu.roll(both[8:16], 1, 0)
        return inside + jnp.where(sub8 == 0, 0.0, edge), jnp.where(sub8 == 0, edge, 0.0)

    for n in (3, 4):
        second[n].wait_recv()
    finish(inner)
    for n in (0, 1, 2):
        second[n].wait_recv()
    finish((0,))
    x_sum = [total([gx[i, j] * fs[i, j] for i in range(7)]) for j in range(8)]
    y_sum = [total([gy[i, j] * fs[i, j] for j in range(8)]) for i in range(7)]
    z_line = []
    for i in range(7):
        terms = [gz[i, j] * fs[i, j] for j in range(8)]
        z_line.append([weigh(terms, q) for q in range(2)])
    y_high = weigh(y_sum, 1)
    plain = [
        hold[2] - weigh(x_sum, 0) + y_high,
        hold[3] - weigh(x_sum, 1) - y_high,
    ]
    cells = [-weigh([z[q] for z in z_line], 1) for q in range(2)]
    sc[0], sc[1] = vertices(plain, cells)
    third = [
        send(sc.at[1], rc.at[1], (dn, sn)),
        send(sc.at[0], rc.at[0], (dn, s)),
    ]
    for n in (5, 6, 7):
        second[n].wait_recv()
    finish((7,))
    first[13].wait_recv()
    x_net = [x_sum[j] + gx[7, j] * fs[7, j] - rxgx[j] * fs[0, j] for j in range(8)]
    y_low = weigh(y_sum + [y_sum[0]], 0)
    plain = [
        hold[0] + weigh(x_net, 0) + y_low,
        hold[1] + weigh(x_net, 1) - y_low,
    ]
    cells = [-weigh([z[q] for z in z_line] + [z_line[0][q]], 0) for q in range(2)]
    own, sc[2] = vertices(plain, cells)
    third.append(send(sc.at[2], rc.at[2], (d, sn)))
    for copy in third:
        copy.wait_recv()
    coarse = own + rc[0] + (rc[1] + rc[2])
    coarse_ref[0] = coarse[:, 0:17]
    for copy in first + second + third:
        copy.wait_send()


def shards(element_load, mobility, metric):
    field = pltpu.VMEM((8, 8, 8, 128), F32)
    hbm = pl.BlockSpec(memory_space=pltpu.HBM)
    vmem = pl.BlockSpec(memory_space=pltpu.VMEM)
    return pl.pallas_call(
        kernel,
        name="smoother",
        out_shape=(
            pltpu.VMEM((1, 8, 8, 8, 128), F32),
            pltpu.VMEM((1, 8, 17), F32),
        ),
        in_specs=[hbm, hbm, hbm, hbm],
        out_specs=(vmem, vmem),
        scratch_shapes=[
            field, field,
            pltpu.VMEM((3, 1, 8, 16), F32),
            pltpu.VMEM((5, 8, 128), F32),
            pltpu.VMEM((5, 256, 256), BF16),
            *[field] * 13,
            pltpu.VMEM((4, 8, 128), F32),
            pltpu.VMEM((2, 2, 8, 128), F32),
            pltpu.VMEM((18, 8, 128), F32),
            pltpu.VMEM((8, 8, 128), F32),
            pltpu.VMEM((2, 8, 128), F32),
            pltpu.VMEM((2, 8, 128), F32),
            pltpu.VMEM((2, 8, 128), F32),
            pltpu.VMEM((2, 8, 128), F32),
            pltpu.VMEM((3, 8, 128), F32),
            pltpu.VMEM((2, 8, 8, 128), F32),
            pltpu.VMEM((2, 8, 8, 128), F32),
            pltpu.VMEM((18, 8, 128), F32),
            pltpu.VMEM((8, 8, 128), F32),
            pltpu.VMEM((2, 2, 8, 128), F32),
            pltpu.VMEM((4, 2, 8, 128), F32),
            pltpu.VMEM((2, 8, 128), F32),
            pltpu.VMEM((2, 8, 8, 128), F32),
            pltpu.VMEM((2, 8, 128), F32),
            pltpu.VMEM((4, 8, 128), F32),
            pltpu.VMEM((3, 8, 128), F32),
            pltpu.SemaphoreType.DMA((4,)),
            pltpu.SemaphoreType.DMA((25,)),
            pltpu.SemaphoreType.DMA((25,)),
        ],
        compiler_params=pltpu.CompilerParams(collective_id=0, has_side_effects=True),
    )(element_load, mobility, metric, jnp.asarray(small_tables()))


def solution(mesh):
    in_specs = (
        P("dom", None, "sub", None, None),
        P("dom", None, "sub", None, None),
        P(None, "dom", "sub", None),
    )
    out_specs = (P("dom", None, "sub", None, None), P("dom", "sub", None))
    return jax.shard_map(shards, mesh=mesh, in_specs=in_specs, out_specs=out_specs, check_vma=False)
```

```python
import jax
import jax.numpy as jnp
import numpy as np
from jax import lax
from jax.experimental import pallas as pl
from jax.experimental.pallas import tpu as pltpu
from jax.sharding import PartitionSpec as P

NODES = np.array(
    [
        -1.0,
        -0.8717401485096066,
        -0.5917001814331423,
        -0.2092992179024789,
        0.2092992179024789,
        0.5917001814331423,
        0.8717401485096066,
        1.0,
    ]
)
WEIGHTS = np.array(
    [
        0.03571428571428571,
        0.2107042271435061,
        0.3411226924835044,
        0.4124587946587038,
        0.4124587946587038,
        0.3411226924835044,
        0.2107042271435061,
        0.03571428571428571,
    ]
)
THETA = 1.65
DELTA = 1.35
RHO_FIRST = DELTA / THETA
RHO_SECOND = 1.0 / (2.0 * THETA / DELTA - RHO_FIRST)
KEEP = float(1.0 + RHO_SECOND * RHO_FIRST)
STEP = float(2.0 * RHO_SECOND / DELTA)
MESH = pl.DeviceIdType.MESH
F32 = jnp.float32
BF16 = jnp.bfloat16


def derivative_table():
    identity = np.eye(8)
    differences = NODES[:, None] - NODES[None, :] + identity
    barycentric = 1.0 / np.prod(differences, axis=1)
    matrix = barycentric[None, :] / barycentric[:, None] / differences
    matrix = matrix * (1.0 - identity)
    row_sums = np.sum(matrix, axis=1)
    return matrix - identity * row_sums[:, None]


DERIV = derivative_table()


def small_tables():
    deriv = DERIV.astype(np.float32).astype(np.float64)
    lower = (1.0 - NODES) / 8.0
    rows = [
        np.broadcast_to(np.tile(WEIGHTS, 16)[None, :], (8, 128)),
        np.tile(deriv.T, (1, 16)),
        np.tile(deriv, (1, 16)),
        np.tile(deriv * deriv, (1, 16)),
        np.broadcast_to(lower[:, None], (8, 128)),
    ]
    return np.stack(rows).astype(np.float32)


def total(terms):
    while len(terms) > 1:
        terms = [a + b for a, b in zip(terms[0::2], terms[1::2])] + (
            [terms[-1]] if len(terms) % 2 else []
        )
    return terms[0]


def apply_line(matrix, v, sign, rows=range(4)):
    even, odd = {}, {}
    for m in range(4):
        x, y = v[m], v[7 - m]
        if x is not None or y is not None:
            even[m] = x if y is None else x + y
            odd[m] = x if y is None else x - y
    out = [None] * 8
    for a in rows:
        with_even = total([float((matrix[a, m] + matrix[a, 7 - m]) / 2) * e for m, e in even.items()])
        with_odd = total([float((matrix[a, m] - matrix[a, 7 - m]) / 2) * o for m, o in odd.items()])
        out[a] = with_odd + with_even
        out[7 - a] = with_odd - with_even if sign < 0 else with_even - with_odd
    return out


def halves(x):
    high = x.astype(BF16)
    low = (x - high.astype(F32)).astype(BF16)
    return high, low


def wide_dot(x, table):
    high, low = halves(x)
    both = jnp.dot(jnp.concatenate([high, low], axis=1), table, preferred_element_type=F32)
    return both[:, :128] + both[:, 128:]


def kernel(
    load_hbm, mob_hbm, met_hbm, tab_hbm,
    press_ref, coarse_ref,
    load_v, mob_v, met_v, tab_v, mats,
    fx, fy, fz, dg, inv, rhs, fs, kv, zz, gx, gy, gz, k0, k7, ky0, ky7,
    hold, sya, sg, sgx, sk, syb, sye, syc, sc,
    rxl, rxd, rxg, rxgx, rya, rca, rk, rxb, ryb, rcb, rc,
    local_sem, send_sem, recv_sem,
):
    d, s = lax.axis_index("dom"), lax.axis_index("sub")
    nd, ns = lax.axis_size("dom"), lax.axis_size("sub")
    dn, dp = lax.rem(d + 1, nd), lax.rem(d + nd - 1, nd)
    sn, sp = lax.rem(s + 1, ns), lax.rem(s + ns - 1, ns)

    barrier = pltpu.get_barrier_semaphore()
    around = [(dp, sp), (dp, sn), (dn, sp), (dn, sn), (dp, s), (dn, s), (d, sp), (d, sn)]
    for device in around:
        pl.semaphore_signal(barrier, inc=1, device_id=device, device_id_type=MESH)
    fetch = [
        pltpu.make_async_copy(met_hbm, met_v, local_sem.at[0]),
        pltpu.make_async_copy(tab_hbm, tab_v, local_sem.at[1]),
    ]
    fetch += [
        pltpu.make_async_copy(mob_hbm.at[0, i], mob_v.at[i], local_sem.at[2 + i]) for i in range(8)
    ]
    fetch.append(pltpu.make_async_copy(load_hbm.at[0], load_v, local_sem.at[10]))
    for copy in fetch:
        copy.start()

    lane = lax.broadcasted_iota(jnp.int32, (8, 128), 1)
    sub8 = lax.broadcasted_iota(jnp.int32, (8, 128), 0)
    to_right = (lane % 8 == 7) & (lane != 127)
    to_left = (lane % 8 == 0) & (lane != 0)

    def z_joined(v):
        moved = jnp.where(to_right, pltpu.roll(v, 127, 1), pltpu.roll(v, 1, 1))
        return v + jnp.where(to_right | to_left, moved, 0.0)

    fetch[0].wait()
    fetch[1].wait()
    big_row = lax.broadcasted_iota(jnp.int32, (128, 128), 0)
    big_lane = lax.broadcasted_iota(jnp.int32, (128, 128), 1)
    same_cell = big_row // 8 == big_lane // 8

    def put_matrix(slot, matrix):
        high, low = halves(matrix)
        mats[slot, 0:128, 0:128] = high
        mats[slot, 0:128, 128:256] = low
        mats[slot, 128:256, 0:128] = high
        mats[slot, 128:256, 128:256] = jnp.zeros((128, 128), BF16)

    def tall(tile):
        return jnp.broadcast_to(tile[None], (16, 8, 128)).reshape(128, 128)

    for slot in range(3):
        put_matrix(slot, jnp.where(same_cell, tall(tab_v[1 + slot]), 0.0))
    lower = tall(tab_v[4])
    at_low, at_high = big_lane == big_row // 8, big_lane == big_row // 8 + 1
    put_matrix(3, jnp.where(at_low, lower, jnp.where(at_high, 0.25 - lower, 0.0)))
    put_matrix(4, jnp.where(at_low, -0.125, jnp.where(at_high, 0.125, 0.0)))

    cell_of = lax.broadcasted_iota(jnp.int32, (16, 128), 1) // 8
    expand = jnp.where(cell_of == lax.broadcasted_iota(jnp.int32, (16, 128), 0), 1.0, 0.0)
    spread = jnp.dot(
        met_v[...].reshape(24, 16), expand.astype(F32),
        preferred_element_type=F32, precision=lax.Precision.HIGHEST,
    ).reshape(3, 8, 128)
    base = [spread[n] * tab_v[0] for n in range(3)]

    for i in range(8):
        fetch[2 + i].wait()
        for j in range(8):
            m = mob_v[i, :, j, :] * float(WEIGHTS[i] * WEIGHTS[j])
            fx[i, j] = m * base[0]
            fy[i, j] = m * base[1]
            fz[i, j] = m * base[2]
            if i == 7:
                sg[j] = m
    sg[8] = base[1]
    sg[9] = base[2]
    squared = (DERIV * DERIV).T

    def z_diagonal(at):
        shape = fz[at].shape
        zz[at] = wide_dot(fz[at].reshape(-1, 128), mats[2]).reshape(shape)

    z_diagonal(slice(0, 1))
    z_diagonal(slice(7, 8))
    z_diagonal((slice(1, 7), 0))
    z_diagonal((slice(1, 7), 7))
    for j in range(8):
        ends = range(4) if j in (0, 7) else (0,)
        line = apply_line(squared, [fx[i, j] for i in range(8)], 1, ends)
        for i in range(8):
            if line[i] is not None:
                dg[i, j] = line[i] + zz[i, j]
        sg[10 + j] = line[7]
    for i in range(8):
        ends = range(4) if i in (0, 7) else (0,)
        line = apply_line(squared, [fy[i, j] for j in range(8)], 1, ends)
        for j in range(8):
            if line[j] is not None:
                dg[i, j] = dg[i, j] + line[j]
    fetch[10].wait()
    sya[0, 0] = load_v[:, 7, 7, :]
    sya[1, 0] = load_v[:, 0, 0, :]
    sya[0, 1] = dg[:, 7, 7, :]
    sya[1, 1] = dg[:, 0, 0, :]

    used = [0]

    def send(src, dst, device):
        n = used[0]
        used[0] += 1
        copy = pltpu.make_async_remote_copy(
            src_ref=src, dst_ref=dst, send_sem=send_sem.at[n], recv_sem=recv_sem.at[n],
            device_id=device, device_id_type=MESH,
        )
        copy.start()
        return copy

    pl.semaphore_wait(barrier, 8)
    first = [
        send(sya.at[0], rca.at[0], (dn, sn)),
        send(sya.at[1], rca.at[1], (dn, sp)),
        send(sya.at[0], rca.at[2], (dp, sn)),
        send(sya.at[1], rca.at[3], (dp, sp)),
        send(sya.at[0], rya.at[0], (d, sn)),
        send(sya.at[1], rya.at[1], (d, sp)),
        send(dg.at[7], rxd.at[0], (dn, s)),
        send(dg.at[0], rxd.at[1], (dp, s)),
        send(load_hbm.at[0, 7], rxl.at[0], (dn, s)),
        send(load_hbm.at[0, 0], rxl.at[1], (dp, s)),
        send(sg, rxg, (dn, s)),
    ]

    inner = range(1, 7)
    rim = [(i, j) for i in range(8) for j in range(8) if i in (0, 7) or j in (0, 7)]
    deep = [(i, j) for i in inner for j in inner]

    def first_step(i, j, load, diag):
        right = z_joined(load)
        inverse = 1.0 / z_joined(diag)
        rhs[i, j] = right
        inv[i, j] = inverse
        fs[i, j] = inverse * right * float(1.0 / THETA)

    def rim_sums(planes_i, local, planes, sides, corners):
        out = {}
        for i in planes_i:
            line = {j: local(i, j) for j in (range(8) if i in (0, 7) else (0, 7))}
            before, after = sides(0, i), sides(1, i)
            if i == 0:
                line = {j: v + planes(0, j) for j, v in line.items()}
                before, after = before + corners(0, 7), after + corners(1, 7)
            if i == 7:
                line = {j: v + planes(1, j) for j, v in line.items()}
                before, after = before + corners(2, 0), after + corners(3, 0)
            low, high = line[0], line[7]
            line[7] = high + jnp.where(sub8 == 7, after, pltpu.roll(low, 7, 0))
            line[0] = low + jnp.where(sub8 == 0, before, pltpu.roll(high, 1, 0))
            for j, v in line.items():
                out[i, j] = v
        return out

    z_diagonal((slice(1, 7), slice(1, 7)))
    for j in inner:
        line = apply_line(squared, [fx[i, j] for i in range(8)], 1, (1, 2, 3))
        for i in inner:
            dg[i, j] = line[i] + zz[i, j]
    for i in inner:
        line = apply_line(squared, [fy[i, j] for j in range(8)], 1, (1, 2, 3))
        for j in inner:
            dg[i, j] = dg[i, j] + line[j]

    for j in range(8):
        line = [fx[a, j] for a in range(8)]
        for i in range(7):
            k7[i, j] = total([float(DERIV[a, i] * DERIV[a, 7]) * line[a] for a in range(8)])
        line = apply_line(DERIV.T / 8.0, line, -1)
        for i in range(8):
            gx[i, j] = line[i]
        sgx[j] = line[7]
        k7[7, j] = jnp.zeros((8, 128), F32)
    sk[0] = k7[:, 7, 7, :]
    sk[1] = k7[:, 0, 0, :]
    first += [
        send(sk.at[0], rk.at[0], (d, sn)),
        send(sk.at[1], rk.at[1], (d, sp)),
        send(sgx, rxgx, (dn, s)),
    ]
    gz[1:7] = wide_dot(fz[1:7].reshape(384, 128), mats[1]).reshape(6, 8, 8, 128)
    for i in range(1, 7):
        line = apply_line(DERIV.T / 8.0, [fy[i, j] for j in range(8)], -1)
        for j in range(8):
            gy[i, j] = line[j]

    for i, j in deep:
        first_step(i, j, load_v[i, :, j, :], dg[i, j])

    def z_part(at):
        shape = fs[at].shape
        flux = wide_dot(fs[at].reshape(-1, 128), mats[0]) * fz[at].reshape(-1, 128)
        zz[at] = wide_dot(flux, mats[1]).reshape(shape)

    def column(line, m, n):
        return total([float(DERIV[a, m] * DERIV[a, n]) * line[a] for a in range(8)])

    z_part((slice(1, 7), slice(1, 7)))
    for j in inner:
        grad = apply_line(DERIV, [None] + [fs[i, j] for i in inner] + [None], -1)
        line = apply_line(DERIV.T, [fx[i, j] * grad[i] for i in range(8)], -1)
        for i in range(8):
            kv[i, j] = line[i]
        line = [fx[a, j] for a in range(8)]
        for i in range(8):
            k0[i, j] = column(line, i, 0)
    for i in inner:
        grad = apply_line(DERIV, [None] + [fs[i, j] for j in inner] + [None], -1)
        line = apply_line(DERIV.T, [fy[i, j] * grad[j] for j in range(8)], -1)
        for j in range(8):
            kv[i, j] = (kv[i, j] + (line[j] + zz[i, j])) if j in inner else line[j]
        line = [fy[i, b] for b in range(8)]
        for j in range(8):
            ky0[i, j] = column(line, j, 0)
            ky7[i, j] = column(line, j, 7)

    def low_high(v):
        plain = total(v)
        slope = total([float(NODES[m]) * (v[m] - v[7 - m]) for m in range(4)])
        return (plain - slope) * 0.125, (plain + slope) * 0.125

    held = [low_high([load_v[i, :, j, :] for i in range(8)]) for j in range(8)]
    held = [low_high([held[j][p] for j in range(8)]) for p in range(2)]
    for p in range(2):
        for q in range(2):
            hold[2 * p + q] = held[p][q]

    wide = lambda row: jnp.broadcast_to(row, (8, 128))

    def start_rim(planes_i):
        loads = rim_sums(
            planes_i,
            lambda i, j: load_v[i, :, j, :],
            lambda side, j: rxl[side, :, j, :],
            lambda side, i: wide(rya[side, 0, i : i + 1, :]),
            lambda slot, i: wide(rca[slot, 0, i : i + 1, :]),
        )
        diags = rim_sums(
            planes_i,
            lambda i, j: dg[i, j],
            lambda side, j: rxd[side, j],
            lambda side, i: wide(rya[side, 1, i : i + 1, :]),
            lambda slot, i: wide(rca[slot, 1, i : i + 1, :]),
        )
        for i, j in loads:
            first_step(i, j, loads[i, j], diags[i, j])

    for n in (4, 5):
        first[n].wait_recv()
    start_rim(inner)
    for n in (0, 1, 6, 8):
        first[n].wait_recv()
    start_rim((0,))
    for j in range(8):
        if j in inner:
            v = fs[0, j]
            for i in range(8):
                kv[i, j] = kv[i, j] + k0[i, j] * v
        else:
            grad = apply_line(DERIV, [fs[i, j] for i in range(7)] + [None], -1)
            line = apply_line(DERIV.T, [fx[i, j] * grad[i] for i in range(8)], -1)
            for i in range(8):
                kv[i, j] = (kv[i, j] + line[i]) if i in inner else line[i]
    sye[0] = kv[:, 7, 7, :]
    sye[1] = kv[:, 0, 0, :]
    second = [
        send(sye.at[0], rcb.at[0], (dn, sn)),
        send(sye.at[1], rcb.at[1], (dn, sp)),
        send(kv.at[7], rxb.at[0], (dn, s)),
    ]

    z_part((slice(1, 7), 0))
    z_part((slice(1, 7), 7))
    for i in inner:
        low, high = fs[i, 0], fs[i, 7]
        for j in range(8):
            value = kv[i, j] + (ky0[i, j] * low + ky7[i, j] * high)
            kv[i, j] = value if j in inner else value + zz[i, j]
    first[10].wait_recv()
    for j in range(8):
        fy[0, j] = fy[0, j] + rxg[j] * rxg[8]
        fz[0, j] = fz[0, j] + rxg[j] * rxg[9]
    z_part(slice(0, 1))
    grad = apply_line(DERIV, [fs[0, j] for j in range(8)], -1)
    line = apply_line(DERIV.T, [fy[0, j] * grad[j] for j in range(8)], -1)
    for j in range(8):
        kv[0, j] = kv[0, j] + rxg[10 + j] * fs[0, j] + (line[j] + zz[0, j])
    syb[0] = kv[:, 7, 7, :]
    syb[1] = kv[:, 0, 0, :]
    second += [send(syb.at[0], ryb.at[0], (d, sn)), send(syb.at[1], ryb.at[1], (d, sp))]

    for n in (2, 3, 7, 9):
        first[n].wait_recv()
    start_rim((7,))
    for j in range(8):
        v = fs[7, j]
        for i in range(7):
            kv[i, j] = kv[i, j] + k7[i, j] * v
    syc[0] = kv[:, 7, 7, :]
    syc[1] = kv[:, 0, 0, :]
    second += [
        send(syc.at[0], rcb.at[2], (dp, sn)),
        send(syc.at[1], rcb.at[3], (dp, sp)),
        send(kv.at[0], rxb.at[1], (dp, s)),
    ]
    gz[0] = wide_dot(fz[0].reshape(64, 128), mats[1]).reshape(8, 8, 128)
    line = apply_line(DERIV.T / 8.0, [fy[0, j] for j in range(8)], -1)
    for j in range(8):
        gy[0, j] = line[j]
    for n in (11, 12):
        first[n].wait_recv()
    ends = [fs[7, 0], fs[7, 7]]

    weight = [[float((1.0 + (2 * p - 1) * NODES[m]) / 8.0) for m in range(8)] for p in range(2)]
    part_x, part_y, part_z = [[] for _ in range(8)], [[] for _ in range(8)], {}

    def smoothed(i, j, value):
        resid = rhs[i, j] - z_joined(value)
        p = KEEP * fs[i, j] + STEP * (inv[i, j] * resid)
        fs[i, j] = p
        press_ref[0, i, :, j, :] = p

    for i, j in deep:
        smoothed(i, j, kv[i, j])

    def finish(planes_i):
        sums = rim_sums(
            planes_i,
            lambda i, j: kv[i, j],
            lambda side, j: rxb[side, j],
            lambda side, i: wide(ryb[side, i : i + 1, :])
            + (wide(rk[side, i : i + 1, :]) * ends[side] if i < 7 else 0.0),
            lambda slot, i: wide(rcb[slot, i : i + 1, :]),
        )
        for (i, j), value in sums.items():
            smoothed(i, j, value)

    def weigh(line, p):
        return total([weight[p][m] * v for m, v in enumerate(line) if weight[p][m] != 0.0])

    def vertices(plain, cells):
        both = wide_dot(jnp.concatenate(plain, axis=0), mats[3]) + wide_dot(
            jnp.concatenate(cells, axis=0), mats[4]
        )
        inside, edge = both[0:8], pltpu.roll(both[8:16], 1, 0)
        return inside + jnp.where(sub8 == 0, 0.0, edge), jnp.where(sub8 == 0, edge, 0.0)

    for n in (3, 4):
        second[n].wait_recv()
    finish(inner)
    for n in (0, 1, 2):
        second[n].wait_recv()
    finish((0,))
    x_sum = [total([gx[i, j] * fs[i, j] for i in range(7)]) for j in range(8)]
    y_sum = [total([gy[i, j] * fs[i, j] for j in range(8)]) for i in range(7)]
    z_line = []
    for i in range(7):
        terms = [gz[i, j] * fs[i, j] for j in range(8)]
        z_line.append([weigh(terms, q) for q in range(2)])
    y_high = weigh(y_sum, 1)
    plain = [
        hold[2] - weigh(x_sum, 0) + y_high,
        hold[3] - weigh(x_sum, 1) - y_high,
    ]
    cells = [-weigh([z[q] for z in z_line], 1) for q in range(2)]
    sc[0], sc[1] = vertices(plain, cells)
    third = [
        send(sc.at[1], rc.at[1], (dn, sn)),
        send(sc.at[0], rc.at[0], (dn, s)),
    ]
    for n in (5, 6, 7):
        second[n].wait_recv()
    finish((7,))
    first[13].wait_recv()
    x_net = [x_sum[j] + gx[7, j] * fs[7, j] - rxgx[j] * fs[0, j] for j in range(8)]
    y_low = weigh(y_sum + [y_sum[0]], 0)
    plain = [
        hold[0] + weigh(x_net, 0) + y_low,
        hold[1] + weigh(x_net, 1) - y_low,
    ]
    cells = [-weigh([z[q] for z in z_line] + [z_line[0][q]], 0) for q in range(2)]
    own, sc[2] = vertices(plain, cells)
    third.append(send(sc.at[2], rc.at[2], (d, sn)))
    for copy in third:
        copy.wait_recv()
    coarse = own + rc[0] + (rc[1] + rc[2])
    coarse_ref[0] = coarse[:, 0:17]
    for copy in first + second + third:
        copy.wait_send()


def write_out(pressure_ref, coarse_ref, pressure_hbm, coarse_hbm, sem):
    copies = [pltpu.make_async_copy(coarse_ref, coarse_hbm, sem.at[8])]
    copies += [
        pltpu.make_async_copy(pressure_ref.at[0, i], pressure_hbm.at[0, i], sem.at[i])
        for i in range(8)
    ]
    for copy in copies:
        copy.start()
    for copy in copies:
        copy.wait()


def shards(element_load, mobility, metric):
    field = pltpu.VMEM((8, 8, 8, 128), F32)
    hbm = pl.BlockSpec(memory_space=pltpu.HBM)
    vmem = pl.BlockSpec(memory_space=pltpu.VMEM)
    pressure, coarse = pl.pallas_call(
        kernel,
        name="smoother",
        out_shape=(
            pltpu.VMEM((1, 8, 8, 8, 128), F32),
            pltpu.VMEM((1, 8, 17), F32),
        ),
        in_specs=[hbm, hbm, hbm, hbm],
        out_specs=(vmem, vmem),
        scratch_shapes=[
            field, field,
            pltpu.VMEM((3, 1, 8, 16), F32),
            pltpu.VMEM((5, 8, 128), F32),
            pltpu.VMEM((5, 256, 256), BF16),
            *[field] * 16,
            pltpu.VMEM((4, 8, 128), F32),
            pltpu.VMEM((2, 2, 8, 128), F32),
            pltpu.VMEM((18, 8, 128), F32),
            pltpu.VMEM((8, 8, 128), F32),
            pltpu.VMEM((2, 8, 128), F32),
            pltpu.VMEM((2, 8, 128), F32),
            pltpu.VMEM((2, 8, 128), F32),
            pltpu.VMEM((2, 8, 128), F32),
            pltpu.VMEM((3, 8, 128), F32),
            pltpu.VMEM((2, 8, 8, 128), F32),
            pltpu.VMEM((2, 8, 8, 128), F32),
            pltpu.VMEM((18, 8, 128), F32),
            pltpu.VMEM((8, 8, 128), F32),
            pltpu.VMEM((2, 2, 8, 128), F32),
            pltpu.VMEM((4, 2, 8, 128), F32),
            pltpu.VMEM((2, 8, 128), F32),
            pltpu.VMEM((2, 8, 8, 128), F32),
            pltpu.VMEM((2, 8, 128), F32),
            pltpu.VMEM((4, 8, 128), F32),
            pltpu.VMEM((3, 8, 128), F32),
            pltpu.SemaphoreType.DMA((11,)),
            pltpu.SemaphoreType.DMA((25,)),
            pltpu.SemaphoreType.DMA((25,)),
        ],
        compiler_params=pltpu.CompilerParams(collective_id=0, has_side_effects=True),
    )(element_load, mobility, metric, jnp.asarray(small_tables()))
    return pl.pallas_call(
        write_out,
        name="write_out",
        out_shape=(
            jax.ShapeDtypeStruct(pressure.shape, F32),
            jax.ShapeDtypeStruct(coarse.shape, F32),
        ),
        in_specs=[vmem, vmem],
        out_specs=(hbm, hbm),
        scratch_shapes=[pltpu.SemaphoreType.DMA((9,))],
    )(
        pltpu.with_memory_space_constraint(pressure, pltpu.VMEM),
        pltpu.with_memory_space_constraint(coarse, pltpu.VMEM),
    )


def solution(mesh):
    in_specs = (
        P("dom", None, "sub", None, None),
        P("dom", None, "sub", None, None),
        P(None, "dom", "sub", None),
    )
    out_specs = (P("dom", None, "sub", None, None), P("dom", "sub", None))
    return jax.shard_map(shards, mesh=mesh, in_specs=in_specs, out_specs=out_specs, check_vma=False)
```

```python
import jax
import jax.numpy as jnp
import numpy as np
from jax import lax
from jax.experimental import pallas as pl
from jax.experimental.pallas import tpu as pltpu
from jax.sharding import PartitionSpec as P

NODES = np.array(
    [
        -1.0,
        -0.8717401485096066,
        -0.5917001814331423,
        -0.2092992179024789,
        0.2092992179024789,
        0.5917001814331423,
        0.8717401485096066,
        1.0,
    ]
)
WEIGHTS = np.array(
    [
        0.03571428571428571,
        0.2107042271435061,
        0.3411226924835044,
        0.4124587946587038,
        0.4124587946587038,
        0.3411226924835044,
        0.2107042271435061,
        0.03571428571428571,
    ]
)
THETA = 1.65
DELTA = 1.35
RHO_FIRST = DELTA / THETA
RHO_SECOND = 1.0 / (2.0 * THETA / DELTA - RHO_FIRST)
KEEP = float(1.0 + RHO_SECOND * RHO_FIRST)
STEP = float(2.0 * RHO_SECOND / DELTA)
MESH = pl.DeviceIdType.MESH
F32 = jnp.float32
BF16 = jnp.bfloat16


def derivative_table():
    identity = np.eye(8)
    differences = NODES[:, None] - NODES[None, :] + identity
    barycentric = 1.0 / np.prod(differences, axis=1)
    matrix = barycentric[None, :] / barycentric[:, None] / differences
    matrix = matrix * (1.0 - identity)
    row_sums = np.sum(matrix, axis=1)
    return matrix - identity * row_sums[:, None]


DERIV = derivative_table()


def small_tables():
    deriv = DERIV.astype(np.float32).astype(np.float64)
    lower = (1.0 - NODES) / 8.0
    rows = [
        np.broadcast_to(np.tile(WEIGHTS, 16)[None, :], (8, 128)),
        np.tile(deriv.T, (1, 16)),
        np.tile(deriv, (1, 16)),
        np.tile(deriv * deriv, (1, 16)),
        np.broadcast_to(lower[:, None], (8, 128)),
    ]
    return np.stack(rows).astype(np.float32)


def total(terms):
    while len(terms) > 1:
        terms = [a + b for a, b in zip(terms[0::2], terms[1::2])] + (
            [terms[-1]] if len(terms) % 2 else []
        )
    return terms[0]


def apply_line(matrix, v, sign, rows=range(4)):
    even, odd = {}, {}
    for m in range(4):
        x, y = v[m], v[7 - m]
        if x is not None or y is not None:
            even[m] = x if y is None else x + y
            odd[m] = x if y is None else x - y
    out = [None] * 8
    for a in rows:
        with_even = total([float((matrix[a, m] + matrix[a, 7 - m]) / 2) * e for m, e in even.items()])
        with_odd = total([float((matrix[a, m] - matrix[a, 7 - m]) / 2) * o for m, o in odd.items()])
        out[a] = with_odd + with_even
        out[7 - a] = with_odd - with_even if sign < 0 else with_even - with_odd
    return out


def halves(x):
    high = x.astype(BF16)
    low = (x - high.astype(F32)).astype(BF16)
    return high, low


def wide_dot(x, table):
    high, low = halves(x)
    both = jnp.dot(jnp.concatenate([high, low], axis=1), table, preferred_element_type=F32)
    return both[:, :128] + both[:, 128:]


def kernel(
    load_hbm, mob_hbm, met_hbm, tab_hbm,
    press_ref, coarse_ref,
    load_v, mob_v, met_v, tab_v, mats,
    fx, fy, fz, dg, inv, rhs, fs, kv, zz, gx, gy, gz, k0, k7, ky0, ky7,
    hold, sya, sca, sg, sgx, sk, syb, sye, syc, sc,
    rxl, rxd, rxg, rxgx, rya, rca, rk, rxb, ryb, rcb, rc,
    local_sem, send_sem, recv_sem,
):
    d, s = lax.axis_index("dom"), lax.axis_index("sub")
    nd, ns = lax.axis_size("dom"), lax.axis_size("sub")
    dn, dp = lax.rem(d + 1, nd), lax.rem(d + nd - 1, nd)
    sn, sp = lax.rem(s + 1, ns), lax.rem(s + ns - 1, ns)

    barrier = pltpu.get_barrier_semaphore()
    around = [(dp, sp), (dp, sn), (dn, sp), (dn, sn), (dp, s), (dn, s), (d, sp), (d, sn)]
    for device in around:
        pl.semaphore_signal(barrier, inc=1, device_id=device, device_id_type=MESH)
    fetch = [
        pltpu.make_async_copy(met_hbm, met_v, local_sem.at[0]),
        pltpu.make_async_copy(tab_hbm, tab_v, local_sem.at[1]),
    ]
    fetch += [
        pltpu.make_async_copy(
            mob_hbm.at[0, pl.ds(4 * h, 4)], mob_v.at[pl.ds(4 * h, 4)], local_sem.at[2 + h]
        )
        for h in range(2)
    ]
    fetch.append(pltpu.make_async_copy(load_hbm.at[0], load_v, local_sem.at[4]))
    for copy in fetch:
        copy.start()

    lane = lax.broadcasted_iota(jnp.int32, (8, 128), 1)
    sub8 = lax.broadcasted_iota(jnp.int32, (8, 128), 0)
    to_right = (lane % 8 == 7) & (lane != 127)
    to_left = (lane % 8 == 0) & (lane != 0)

    def z_joined(v):
        moved = jnp.where(to_right, pltpu.roll(v, 127, 1), pltpu.roll(v, 1, 1))
        return v + jnp.where(to_right | to_left, moved, 0.0)

    fetch[0].wait()
    fetch[1].wait()
    big_row = lax.broadcasted_iota(jnp.int32, (128, 128), 0)
    big_lane = lax.broadcasted_iota(jnp.int32, (128, 128), 1)
    same_cell = big_row // 8 == big_lane // 8

    def put_matrix(slot, matrix):
        high, low = halves(matrix)
        mats[slot, 0:128, 0:128] = high
        mats[slot, 0:128, 128:256] = low
        mats[slot, 128:256, 0:128] = high
        mats[slot, 128:256, 128:256] = jnp.zeros((128, 128), BF16)

    def tall(tile):
        return jnp.broadcast_to(tile[None], (16, 8, 128)).reshape(128, 128)

    for slot in range(3):
        put_matrix(slot, jnp.where(same_cell, tall(tab_v[1 + slot]), 0.0))
    lower = tall(tab_v[4])
    at_low, at_high = big_lane == big_row // 8, big_lane == big_row // 8 + 1
    put_matrix(3, jnp.where(at_low, lower, jnp.where(at_high, 0.25 - lower, 0.0)))
    put_matrix(4, jnp.where(at_low, -0.125, jnp.where(at_high, 0.125, 0.0)))

    cell_of = lax.broadcasted_iota(jnp.int32, (16, 128), 1) // 8
    expand = jnp.where(cell_of == lax.broadcasted_iota(jnp.int32, (16, 128), 0), 1.0, 0.0)
    spread = jnp.dot(
        met_v[...].reshape(24, 16), expand.astype(F32),
        preferred_element_type=F32, precision=lax.Precision.HIGHEST,
    ).reshape(3, 8, 128)
    base = [spread[n] * tab_v[0] for n in range(3)]

    for i in range(8):
        if i % 4 == 0:
            fetch[2 + i // 4].wait()
        for j in range(8):
            m = mob_v[i, :, j, :] * float(WEIGHTS[i] * WEIGHTS[j])
            fx[i, j] = m * base[0]
            fy[i, j] = m * base[1]
            fz[i, j] = m * base[2]
            if i == 7:
                sg[j] = m
    sg[8] = base[1]
    sg[9] = base[2]
    squared = (DERIV * DERIV).T

    def z_diagonal(at):
        shape = fz[at].shape
        zz[at] = wide_dot(fz[at].reshape(-1, 128), mats[2]).reshape(shape)

    z_diagonal(slice(0, 1))
    z_diagonal(slice(7, 8))
    z_diagonal((slice(1, 7), 0))
    z_diagonal((slice(1, 7), 7))
    for j in range(8):
        ends = range(4) if j in (0, 7) else (0,)
        line = apply_line(squared, [fx[i, j] for i in range(8)], 1, ends)
        for i in range(8):
            if line[i] is not None:
                dg[i, j] = line[i] + zz[i, j]
        sg[10 + j] = line[7]
    for i in range(8):
        ends = range(4) if i in (0, 7) else (0,)
        line = apply_line(squared, [fy[i, j] for j in range(8)], 1, ends)
        for j in range(8):
            if line[j] is not None:
                dg[i, j] = dg[i, j] + line[j]
    fetch[4].wait()
    sya[0, 0] = load_v[:, 7, 7, :]
    sya[1, 0] = load_v[:, 0, 0, :]
    sya[0, 1] = dg[:, 7, 7, :]
    sya[1, 1] = dg[:, 0, 0, :]
    for slot, (end, i) in enumerate(((0, 7), (1, 7), (0, 0), (1, 0))):
        for field in range(2):
            sca[slot, field : field + 1] = sya[end, field, i : i + 1]

    used = [0]

    def send(src, dst, device):
        n = used[0]
        used[0] += 1
        copy = pltpu.make_async_remote_copy(
            src_ref=src, dst_ref=dst, send_sem=send_sem.at[n], recv_sem=recv_sem.at[n],
            device_id=device, device_id_type=MESH,
        )
        copy.start()
        return copy

    pl.semaphore_wait(barrier, 8)
    first = [
        send(sca.at[0], rca.at[0], (dn, sn)),
        send(sca.at[1], rca.at[1], (dn, sp)),
        send(sca.at[2], rca.at[2], (dp, sn)),
        send(sca.at[3], rca.at[3], (dp, sp)),
        send(sya.at[0], rya.at[0], (d, sn)),
        send(sya.at[1], rya.at[1], (d, sp)),
        send(dg.at[7], rxd.at[0], (dn, s)),
        send(dg.at[0], rxd.at[1], (dp, s)),
        send(load_hbm.at[0, 7], rxl.at[0], (dn, s)),
        send(load_hbm.at[0, 0], rxl.at[1], (dp, s)),
        send(sg, rxg, (dn, s)),
    ]

    inner = range(1, 7)
    rim = [(i, j) for i in range(8) for j in range(8) if i in (0, 7) or j in (0, 7)]
    deep = [(i, j) for i in inner for j in inner]

    def first_step(i, j, load, diag):
        right = z_joined(load)
        inverse = 1.0 / z_joined(diag)
        rhs[i, j] = right
        inv[i, j] = inverse
        fs[i, j] = inverse * right * float(1.0 / THETA)

    def rim_sums(planes_i, local, planes, sides, corners):
        out = {}
        for i in planes_i:
            line = {j: local(i, j) for j in (range(8) if i in (0, 7) else (0, 7))}
            before, after = sides(0, i), sides(1, i)
            if i == 0:
                line = {j: v + planes(0, j) for j, v in line.items()}
                before, after = before + corners(0, 7), after + corners(1, 7)
            if i == 7:
                line = {j: v + planes(1, j) for j, v in line.items()}
                before, after = before + corners(2, 0), after + corners(3, 0)
            low, high = line[0], line[7]
            line[7] = high + jnp.where(sub8 == 7, after, pltpu.roll(low, 7, 0))
            line[0] = low + jnp.where(sub8 == 0, before, pltpu.roll(high, 1, 0))
            for j, v in line.items():
                out[i, j] = v
        return out

    z_diagonal((slice(1, 7), slice(1, 7)))
    for j in inner:
        line = apply_line(squared, [fx[i, j] for i in range(8)], 1, (1, 2, 3))
        for i in inner:
            dg[i, j] = line[i] + zz[i, j]
    for i in inner:
        line = apply_line(squared, [fy[i, j] for j in range(8)], 1, (1, 2, 3))
        for j in inner:
            dg[i, j] = dg[i, j] + line[j]

    for j in range(8):
        line = [fx[a, j] for a in range(8)]
        for i in range(7):
            k7[i, j] = total([float(DERIV[a, i] * DERIV[a, 7]) * line[a] for a in range(8)])
        line = apply_line(DERIV.T / 8.0, line, -1)
        for i in range(8):
            gx[i, j] = line[i]
        sgx[j] = line[7]
        k7[7, j] = jnp.zeros((8, 128), F32)
    sk[0] = k7[:, 7, 7, :]
    sk[1] = k7[:, 0, 0, :]
    first += [
        send(sk.at[0], rk.at[0], (d, sn)),
        send(sk.at[1], rk.at[1], (d, sp)),
        send(sgx, rxgx, (dn, s)),
    ]
    gz[1:7] = wide_dot(fz[1:7].reshape(384, 128), mats[1]).reshape(6, 8, 8, 128)
    for i in range(1, 7):
        line = apply_line(DERIV.T / 8.0, [fy[i, j] for j in range(8)], -1)
        for j in range(8):
            gy[i, j] = line[j]

    for i, j in deep:
        first_step(i, j, load_v[i, :, j, :], dg[i, j])

    def z_part(at):
        shape = fs[at].shape
        flux = wide_dot(fs[at].reshape(-1, 128), mats[0]) * fz[at].reshape(-1, 128)
        zz[at] = wide_dot(flux, mats[1]).reshape(shape)

    def column(line, m, n):
        return total([float(DERIV[a, m] * DERIV[a, n]) * line[a] for a in range(8)])

    z_part((slice(1, 7), slice(1, 7)))
    for j in inner:
        grad = apply_line(DERIV, [None] + [fs[i, j] for i in inner] + [None], -1)
        line = apply_line(DERIV.T, [fx[i, j] * grad[i] for i in range(8)], -1)
        for i in range(8):
            kv[i, j] = line[i]
        line = [fx[a, j] for a in range(8)]
        for i in range(8):
            k0[i, j] = column(line, i, 0)
    for i in inner:
        grad = apply_line(DERIV, [None] + [fs[i, j] for j in inner] + [None], -1)
        line = apply_line(DERIV.T, [fy[i, j] * grad[j] for j in range(8)], -1)
        for j in range(8):
            kv[i, j] = (kv[i, j] + (line[j] + zz[i, j])) if j in inner else line[j]
        line = [fy[i, b] for b in range(8)]
        for j in range(8):
            ky0[i, j] = column(line, j, 0)
            ky7[i, j] = column(line, j, 7)

    def low_high(v):
        plain = total(v)
        slope = total([float(NODES[m]) * (v[m] - v[7 - m]) for m in range(4)])
        return (plain - slope) * 0.125, (plain + slope) * 0.125

    held = [low_high([load_v[i, :, j, :] for i in range(8)]) for j in range(8)]
    held = [low_high([held[j][p] for j in range(8)]) for p in range(2)]
    for p in range(2):
        for q in range(2):
            hold[2 * p + q] = held[p][q]

    wide = lambda row: jnp.broadcast_to(row, (8, 128))

    def start_rim(planes_i):
        loads = rim_sums(
            planes_i,
            lambda i, j: load_v[i, :, j, :],
            lambda side, j: rxl[side, :, j, :],
            lambda side, i: wide(rya[side, 0, i : i + 1, :]),
            lambda slot, i: wide(rca[slot, 0:1, :]),
        )
        diags = rim_sums(
            planes_i,
            lambda i, j: dg[i, j],
            lambda side, j: rxd[side, j],
            lambda side, i: wide(rya[side, 1, i : i + 1, :]),
            lambda slot, i: wide(rca[slot, 1:2, :]),
        )
        for i, j in loads:
            first_step(i, j, loads[i, j], diags[i, j])

    for n in (4, 5, 6, 8, 0, 1):
        first[n].wait_recv()
    start_rim(range(7))
    for j in range(8):
        if j in inner:
            v = fs[0, j]
            for i in range(8):
                kv[i, j] = kv[i, j] + k0[i, j] * v
        else:
            grad = apply_line(DERIV, [fs[i, j] for i in range(7)] + [None], -1)
            line = apply_line(DERIV.T, [fx[i, j] * grad[i] for i in range(8)], -1)
            for i in range(8):
                kv[i, j] = (kv[i, j] + line[i]) if i in inner else line[i]
    sye[0] = kv[:, 7, 7, :]
    sye[1] = kv[:, 0, 0, :]
    second = [
        send(sye.at[0], rcb.at[0], (dn, sn)),
        send(sye.at[1], rcb.at[1], (dn, sp)),
        send(kv.at[7], rxb.at[0], (dn, s)),
    ]

    z_part((slice(1, 7), 0))
    z_part((slice(1, 7), 7))
    for i in inner:
        low, high = fs[i, 0], fs[i, 7]
        for j in range(8):
            value = kv[i, j] + (ky0[i, j] * low + ky7[i, j] * high)
            kv[i, j] = value if j in inner else value + zz[i, j]
    first[10].wait_recv()
    for j in range(8):
        fy[0, j] = fy[0, j] + rxg[j] * rxg[8]
        fz[0, j] = fz[0, j] + rxg[j] * rxg[9]
    z_part(slice(0, 1))
    grad = apply_line(DERIV, [fs[0, j] for j in range(8)], -1)
    line = apply_line(DERIV.T, [fy[0, j] * grad[j] for j in range(8)], -1)
    for j in range(8):
        kv[0, j] = kv[0, j] + rxg[10 + j] * fs[0, j] + (line[j] + zz[0, j])
    syb[0] = kv[:, 7, 7, :]
    syb[1] = kv[:, 0, 0, :]
    second += [send(syb.at[0], ryb.at[0], (d, sn)), send(syb.at[1], ryb.at[1], (d, sp))]

    for n in (2, 3, 7, 9):
        first[n].wait_recv()
    start_rim((7,))
    for j in range(8):
        v = fs[7, j]
        for i in range(7):
            kv[i, j] = kv[i, j] + k7[i, j] * v
    syc[0] = kv[:, 7, 7, :]
    syc[1] = kv[:, 0, 0, :]
    second += [
        send(syc.at[0], rcb.at[2], (dp, sn)),
        send(syc.at[1], rcb.at[3], (dp, sp)),
        send(kv.at[0], rxb.at[1], (dp, s)),
    ]
    gz[0] = wide_dot(fz[0].reshape(64, 128), mats[1]).reshape(8, 8, 128)
    line = apply_line(DERIV.T / 8.0, [fy[0, j] for j in range(8)], -1)
    for j in range(8):
        gy[0, j] = line[j]
    for n in (11, 12):
        first[n].wait_recv()
    ends = [fs[7, 0], fs[7, 7]]

    weight = [[float((1.0 + (2 * p - 1) * NODES[m]) / 8.0) for m in range(8)] for p in range(2)]
    part_x, part_y, part_z = [[] for _ in range(8)], [[] for _ in range(8)], {}

    def smoothed(i, j, value):
        resid = rhs[i, j] - z_joined(value)
        p = KEEP * fs[i, j] + STEP * (inv[i, j] * resid)
        fs[i, j] = p
        press_ref[0, i, :, j, :] = p

    for i, j in deep:
        smoothed(i, j, kv[i, j])

    def finish(planes_i):
        sums = rim_sums(
            planes_i,
            lambda i, j: kv[i, j],
            lambda side, j: rxb[side, j],
            lambda side, i: wide(ryb[side, i : i + 1, :])
            + (wide(rk[side, i : i + 1, :]) * ends[side] if i < 7 else 0.0),
            lambda slot, i: wide(rcb[slot, i : i + 1, :]),
        )
        for (i, j), value in sums.items():
            smoothed(i, j, value)

    def weigh(line, p):
        return total([weight[p][m] * v for m, v in enumerate(line) if weight[p][m] != 0.0])

    def vertices(plain, cells):
        both = wide_dot(jnp.concatenate(plain, axis=0), mats[3]) + wide_dot(
            jnp.concatenate(cells, axis=0), mats[4]
        )
        inside, edge = both[0:8], pltpu.roll(both[8:16], 1, 0)
        return inside + jnp.where(sub8 == 0, 0.0, edge), jnp.where(sub8 == 0, edge, 0.0)

    x_deep = {j: total([gx[i, j] * fs[i, j] for i in inner]) for j in inner}
    y_deep = {i: total([gy[i, j] * fs[i, j] for j in inner]) for i in inner}
    z_deep = {}
    for i in inner:
        terms = {j: gz[i, j] * fs[i, j] for j in inner}
        z_deep[i] = [total([weight[q][j] * v for j, v in terms.items()]) for q in range(2)]
    for n in (2, 0, 1, 3, 4):
        second[n].wait_recv()
    finish(range(7))
    x_sum, y_sum, z_line = [], [], []
    for j in range(8):
        deep_part = x_deep[j] if j in inner else total([gx[i, j] * fs[i, j] for i in inner])
        x_sum.append(deep_part + gx[0, j] * fs[0, j])
    for i in range(7):
        if i in inner:
            low, high = gz[i, 0] * fs[i, 0], gz[i, 7] * fs[i, 7]
            y_sum.append(y_deep[i] + (gy[i, 0] * fs[i, 0] + gy[i, 7] * fs[i, 7]))
            z_line.append([z_deep[i][0] + 0.25 * low, z_deep[i][1] + 0.25 * high])
        else:
            y_sum.append(total([gy[i, j] * fs[i, j] for j in range(8)]))
            terms = [gz[i, j] * fs[i, j] for j in range(8)]
            z_line.append([weigh(terms, q) for q in range(2)])
    y_high = weigh(y_sum, 1)
    plain = [
        hold[2] - weigh(x_sum, 0) + y_high,
        hold[3] - weigh(x_sum, 1) - y_high,
    ]
    cells = [-weigh([z[q] for z in z_line], 1) for q in range(2)]
    sc[0], sc[1] = vertices(plain, cells)
    third = [
        send(sc.at[1], rc.at[1], (dn, sn)),
        send(sc.at[0], rc.at[0], (dn, s)),
    ]
    for n in (5, 6, 7):
        second[n].wait_recv()
    finish((7,))
    first[13].wait_recv()
    x_net = [x_sum[j] + gx[7, j] * fs[7, j] - rxgx[j] * fs[0, j] for j in range(8)]
    y_low = weigh(y_sum + [y_sum[0]], 0)
    plain = [
        hold[0] + weigh(x_net, 0) + y_low,
        hold[1] + weigh(x_net, 1) - y_low,
    ]
    cells = [-weigh([z[q] for z in z_line] + [z_line[0][q]], 0) for q in range(2)]
    own, sc[2] = vertices(plain, cells)
    third.append(send(sc.at[2], rc.at[2], (d, sn)))
    for copy in third:
        copy.wait_recv()
    coarse = own + rc[0] + (rc[1] + rc[2])
    coarse_ref[0] = coarse[:, 0:17]
    for copy in first + second + third:
        copy.wait_send()


def write_out(pressure_ref, coarse_ref, pressure_hbm, coarse_hbm, sem):
    copies = [pltpu.make_async_copy(coarse_ref, coarse_hbm, sem.at[8])]
    copies += [
        pltpu.make_async_copy(pressure_ref.at[0, i], pressure_hbm.at[0, i], sem.at[i])
        for i in range(8)
    ]
    for copy in copies:
        copy.start()
    for copy in copies:
        copy.wait()


def shards(element_load, mobility, metric):
    field = pltpu.VMEM((8, 8, 8, 128), F32)
    hbm = pl.BlockSpec(memory_space=pltpu.HBM)
    vmem = pl.BlockSpec(memory_space=pltpu.VMEM)
    pressure, coarse = pl.pallas_call(
        kernel,
        name="smoother",
        out_shape=(
            pltpu.VMEM((1, 8, 8, 8, 128), F32),
            pltpu.VMEM((1, 8, 17), F32),
        ),
        in_specs=[hbm, hbm, hbm, hbm],
        out_specs=(vmem, vmem),
        scratch_shapes=[
            field, field,
            pltpu.VMEM((3, 1, 8, 16), F32),
            pltpu.VMEM((5, 8, 128), F32),
            pltpu.VMEM((5, 256, 256), BF16),
            *[field] * 16,
            pltpu.VMEM((4, 8, 128), F32),
            pltpu.VMEM((2, 2, 8, 128), F32),
            pltpu.VMEM((4, 2, 128), F32),
            pltpu.VMEM((18, 8, 128), F32),
            pltpu.VMEM((8, 8, 128), F32),
            pltpu.VMEM((2, 8, 128), F32),
            pltpu.VMEM((2, 8, 128), F32),
            pltpu.VMEM((2, 8, 128), F32),
            pltpu.VMEM((2, 8, 128), F32),
            pltpu.VMEM((3, 8, 128), F32),
            pltpu.VMEM((2, 8, 8, 128), F32),
            pltpu.VMEM((2, 8, 8, 128), F32),
            pltpu.VMEM((18, 8, 128), F32),
            pltpu.VMEM((8, 8, 128), F32),
            pltpu.VMEM((2, 2, 8, 128), F32),
            pltpu.VMEM((4, 2, 128), F32),
            pltpu.VMEM((2, 8, 128), F32),
            pltpu.VMEM((2, 8, 8, 128), F32),
            pltpu.VMEM((2, 8, 128), F32),
            pltpu.VMEM((4, 8, 128), F32),
            pltpu.VMEM((3, 8, 128), F32),
            pltpu.SemaphoreType.DMA((5,)),
            pltpu.SemaphoreType.DMA((25,)),
            pltpu.SemaphoreType.DMA((25,)),
        ],
        compiler_params=pltpu.CompilerParams(collective_id=0, has_side_effects=True),
    )(element_load, mobility, metric, jnp.asarray(small_tables()))
    return pl.pallas_call(
        write_out,
        name="write_out",
        out_shape=(
            jax.ShapeDtypeStruct(pressure.shape, F32),
            jax.ShapeDtypeStruct(coarse.shape, F32),
        ),
        in_specs=[vmem, vmem],
        out_specs=(hbm, hbm),
        scratch_shapes=[pltpu.SemaphoreType.DMA((9,))],
    )(
        pltpu.with_memory_space_constraint(pressure, pltpu.VMEM),
        pltpu.with_memory_space_constraint(coarse, pltpu.VMEM),
    )


def solution(mesh):
    in_specs = (
        P("dom", None, "sub", None, None),
        P("dom", None, "sub", None, None),
        P(None, "dom", "sub", None),
    )
    out_specs = (P("dom", None, "sub", None, None), P("dom", "sub", None))
    return jax.shard_map(shards, mesh=mesh, in_specs=in_specs, out_specs=out_specs, check_vma=False)
```

```python
import jax
import jax.numpy as jnp
import numpy as np
from jax import lax
from jax.experimental import pallas as pl
from jax.experimental.pallas import tpu as pltpu
from jax.sharding import PartitionSpec as P

NODES = np.array(
    [
        -1.0,
        -0.8717401485096066,
        -0.5917001814331423,
        -0.2092992179024789,
        0.2092992179024789,
        0.5917001814331423,
        0.8717401485096066,
        1.0,
    ]
)
WEIGHTS = np.array(
    [
        0.03571428571428571,
        0.2107042271435061,
        0.3411226924835044,
        0.4124587946587038,
        0.4124587946587038,
        0.3411226924835044,
        0.2107042271435061,
        0.03571428571428571,
    ]
)
THETA = 1.65
DELTA = 1.35
RHO_FIRST = DELTA / THETA
RHO_SECOND = 1.0 / (2.0 * THETA / DELTA - RHO_FIRST)
KEEP = float(1.0 + RHO_SECOND * RHO_FIRST)
STEP = float(2.0 * RHO_SECOND / DELTA)
MESH = pl.DeviceIdType.MESH
F32 = jnp.float32
BF16 = jnp.bfloat16


def derivative_table():
    identity = np.eye(8)
    differences = NODES[:, None] - NODES[None, :] + identity
    barycentric = 1.0 / np.prod(differences, axis=1)
    matrix = barycentric[None, :] / barycentric[:, None] / differences
    matrix = matrix * (1.0 - identity)
    row_sums = np.sum(matrix, axis=1)
    return matrix - identity * row_sums[:, None]


DERIV = derivative_table()


def small_tables():
    deriv = DERIV.astype(np.float32).astype(np.float64)
    lower = (1.0 - NODES) / 8.0
    rows = [
        np.broadcast_to(np.tile(WEIGHTS, 16)[None, :], (8, 128)),
        np.tile(deriv.T, (1, 16)),
        np.tile(deriv, (1, 16)),
        np.tile(deriv * deriv, (1, 16)),
        np.broadcast_to(lower[:, None], (8, 128)),
    ]
    return np.stack(rows).astype(np.float32)


def total(terms):
    while len(terms) > 1:
        terms = [a + b for a, b in zip(terms[0::2], terms[1::2])] + (
            [terms[-1]] if len(terms) % 2 else []
        )
    return terms[0]


def apply_line(matrix, v, sign, rows=range(4)):
    even, odd = {}, {}
    for m in range(4):
        x, y = v[m], v[7 - m]
        if x is not None or y is not None:
            even[m] = x if y is None else x + y
            odd[m] = x if y is None else x - y
    out = [None] * 8
    for a in rows:
        with_even = total([float((matrix[a, m] + matrix[a, 7 - m]) / 2) * e for m, e in even.items()])
        with_odd = total([float((matrix[a, m] - matrix[a, 7 - m]) / 2) * o for m, o in odd.items()])
        out[a] = with_odd + with_even
        out[7 - a] = with_odd - with_even if sign < 0 else with_even - with_odd
    return out


def halves(x):
    high = x.astype(BF16)
    low = (x - high.astype(F32)).astype(BF16)
    return high, low


def wide_dot(x, table):
    high, low = halves(x)
    both = jnp.dot(jnp.concatenate([high, low], axis=1), table, preferred_element_type=F32)
    return both[:, :128] + both[:, 128:]


def kernel(
    load_hbm, mob_hbm, met_hbm, tab_hbm,
    press_ref, coarse_ref,
    load_v, mob_v, met_v, tab_v, mats,
    fx, fy, fz, dg, inv, rhs, fs, kv, zz, gx, gy, gz, k0, k7, ky0, ky7,
    hold, sya, sca, sg, sgx, sk, syb, sye, syc, sc,
    rxl, rxd, rxg, rxgx, rya, rca, rk, rxb, ryb, rcb, rc,
    local_sem, send_sem, recv_sem,
):
    d, s = lax.axis_index("dom"), lax.axis_index("sub")
    nd, ns = lax.axis_size("dom"), lax.axis_size("sub")
    dn, dp = lax.rem(d + 1, nd), lax.rem(d + nd - 1, nd)
    sn, sp = lax.rem(s + 1, ns), lax.rem(s + ns - 1, ns)

    barrier = pltpu.get_barrier_semaphore()
    around = [(dp, sp), (dp, sn), (dn, sp), (dn, sn), (dp, s), (dn, s), (d, sp), (d, sn)]
    for device in around:
        pl.semaphore_signal(barrier, inc=1, device_id=device, device_id_type=MESH)
    fetch = [
        pltpu.make_async_copy(met_hbm, met_v, local_sem.at[0]),
        pltpu.make_async_copy(tab_hbm, tab_v, local_sem.at[1]),
    ]
    fetch += [
        pltpu.make_async_copy(
            mob_hbm.at[0, pl.ds(4 * h, 4)], mob_v.at[pl.ds(4 * h, 4)], local_sem.at[2 + h]
        )
        for h in range(2)
    ]
    fetch.append(pltpu.make_async_copy(load_hbm.at[0], load_v, local_sem.at[4]))
    for copy in fetch:
        copy.start()

    lane = lax.broadcasted_iota(jnp.int32, (8, 128), 1)
    sub8 = lax.broadcasted_iota(jnp.int32, (8, 128), 0)
    to_right = (lane % 8 == 7) & (lane != 127)
    to_left = (lane % 8 == 0) & (lane != 0)

    def z_joined(v):
        moved = jnp.where(to_right, pltpu.roll(v, 127, 1), pltpu.roll(v, 1, 1))
        return v + jnp.where(to_right | to_left, moved, 0.0)

    fetch[0].wait()
    fetch[1].wait()
    big_row = lax.broadcasted_iota(jnp.int32, (128, 128), 0)
    big_lane = lax.broadcasted_iota(jnp.int32, (128, 128), 1)
    same_cell = big_row // 8 == big_lane // 8

    def put_matrix(slot, matrix):
        high, low = halves(matrix)
        mats[slot, 0:128, 0:128] = high
        mats[slot, 0:128, 128:256] = low
        mats[slot, 128:256, 0:128] = high
        mats[slot, 128:256, 128:256] = jnp.zeros((128, 128), BF16)

    def tall(tile):
        return jnp.broadcast_to(tile[None], (16, 8, 128)).reshape(128, 128)

    for slot in range(3):
        put_matrix(slot, jnp.where(same_cell, tall(tab_v[1 + slot]), 0.0))
    lower = tall(tab_v[4])
    at_low, at_high = big_lane == big_row // 8, big_lane == big_row // 8 + 1
    put_matrix(3, jnp.where(at_low, lower, jnp.where(at_high, 0.25 - lower, 0.0)))
    put_matrix(4, jnp.where(at_low, -0.125, jnp.where(at_high, 0.125, 0.0)))

    cell_of = lax.broadcasted_iota(jnp.int32, (16, 128), 1) // 8
    expand = jnp.where(cell_of == lax.broadcasted_iota(jnp.int32, (16, 128), 0), 1.0, 0.0)
    spread = jnp.dot(
        met_v[...].reshape(24, 16), expand.astype(F32),
        preferred_element_type=F32, precision=lax.Precision.HIGHEST,
    ).reshape(3, 8, 128)
    base = [spread[n] * tab_v[0] for n in range(3)]

    for i in range(8):
        if i % 4 == 0:
            fetch[2 + i // 4].wait()
        for j in range(8):
            m = mob_v[i, :, j, :] * float(WEIGHTS[i] * WEIGHTS[j])
            fx[i, j] = m * base[0]
            fy[i, j] = m * base[1]
            fz[i, j] = m * base[2]
            if i == 7:
                sg[j] = m
    sg[8] = base[1]
    sg[9] = base[2]
    squared = (DERIV * DERIV).T

    def z_diagonal(at):
        shape = fz[at].shape
        zz[at] = wide_dot(fz[at].reshape(-1, 128), mats[2]).reshape(shape)

    z_diagonal(slice(0, 1))
    z_diagonal(slice(7, 8))
    z_diagonal((slice(1, 7), 0))
    z_diagonal((slice(1, 7), 7))
    for j in range(8):
        ends = range(4) if j in (0, 7) else (0,)
        line = apply_line(squared, [fx[i, j] for i in range(8)], 1, ends)
        for i in range(8):
            if line[i] is not None:
                dg[i, j] = line[i] + zz[i, j]
        sg[10 + j] = line[7]
    for i in range(8):
        ends = range(4) if i in (0, 7) else (0,)
        line = apply_line(squared, [fy[i, j] for j in range(8)], 1, ends)
        for j in range(8):
            if line[j] is not None:
                dg[i, j] = dg[i, j] + line[j]
    fetch[4].wait()
    sya[0, 0] = load_v[:, 7, 7, :]
    sya[1, 0] = load_v[:, 0, 0, :]
    sya[0, 1] = dg[:, 7, 7, :]
    sya[1, 1] = dg[:, 0, 0, :]
    for slot, (end, i) in enumerate(((0, 7), (1, 7), (0, 0), (1, 0))):
        for field in range(2):
            sca[slot, field : field + 1] = sya[end, field, i : i + 1]

    used = [0]

    def send(src, dst, device):
        n = used[0]
        used[0] += 1
        copy = pltpu.make_async_remote_copy(
            src_ref=src, dst_ref=dst, send_sem=send_sem.at[n], recv_sem=recv_sem.at[n],
            device_id=device, device_id_type=MESH,
        )
        copy.start()
        return copy

    pl.semaphore_wait(barrier, 8)
    sent = {
        0: send(sca.at[0], rca.at[0], (dn, sn)),
        1: send(sca.at[1], rca.at[1], (dn, sp)),
        4: send(sya.at[0], rya.at[0], (d, sn)),
        5: send(sya.at[1], rya.at[1], (d, sp)),
        6: send(dg.at[7], rxd.at[0], (dn, s)),
        8: send(load_hbm.at[0, 7], rxl.at[0], (dn, s)),
        2: send(sca.at[2], rca.at[2], (dp, sn)),
        3: send(sca.at[3], rca.at[3], (dp, sp)),
        10: send(sg, rxg, (dn, s)),
        7: send(dg.at[0], rxd.at[1], (dp, s)),
        9: send(load_hbm.at[0, 0], rxl.at[1], (dp, s)),
    }
    first = [sent[n] for n in range(11)]

    inner = range(1, 7)
    rim = [(i, j) for i in range(8) for j in range(8) if i in (0, 7) or j in (0, 7)]
    deep = [(i, j) for i in inner for j in inner]

    def first_step(i, j, load, diag):
        right = z_joined(load)
        inverse = 1.0 / z_joined(diag)
        rhs[i, j] = right
        inv[i, j] = inverse
        fs[i, j] = inverse * right * float(1.0 / THETA)

    def rim_sums(planes_i, local, planes, sides, corners):
        out = {}
        for i in planes_i:
            line = {j: local(i, j) for j in (range(8) if i in (0, 7) else (0, 7))}
            before, after = sides(0, i), sides(1, i)
            if i == 0:
                line = {j: v + planes(0, j) for j, v in line.items()}
                before, after = before + corners(0, 7), after + corners(1, 7)
            if i == 7:
                line = {j: v + planes(1, j) for j, v in line.items()}
                before, after = before + corners(2, 0), after + corners(3, 0)
            low, high = line[0], line[7]
            line[7] = high + jnp.where(sub8 == 7, after, pltpu.roll(low, 7, 0))
            line[0] = low + jnp.where(sub8 == 0, before, pltpu.roll(high, 1, 0))
            for j, v in line.items():
                out[i, j] = v
        return out

    z_diagonal((slice(1, 7), slice(1, 7)))
    for j in inner:
        line = apply_line(squared, [fx[i, j] for i in range(8)], 1, (1, 2, 3))
        for i in inner:
            dg[i, j] = line[i] + zz[i, j]
    for i in inner:
        line = apply_line(squared, [fy[i, j] for j in range(8)], 1, (1, 2, 3))
        for j in inner:
            dg[i, j] = dg[i, j] + line[j]

    for j in range(8):
        line = [fx[a, j] for a in range(8)]
        for i in range(7):
            k7[i, j] = total([float(DERIV[a, i] * DERIV[a, 7]) * line[a] for a in range(8)])
        line = apply_line(DERIV.T / 8.0, line, -1)
        for i in range(8):
            gx[i, j] = line[i]
        sgx[j] = line[7]
        k7[7, j] = jnp.zeros((8, 128), F32)
    sk[0] = k7[:, 7, 7, :]
    sk[1] = k7[:, 0, 0, :]
    first += [
        send(sk.at[0], rk.at[0], (d, sn)),
        send(sk.at[1], rk.at[1], (d, sp)),
        send(sgx, rxgx, (dn, s)),
    ]
    gz[1:7] = wide_dot(fz[1:7].reshape(384, 128), mats[1]).reshape(6, 8, 8, 128)
    for i in range(1, 7):
        line = apply_line(DERIV.T / 8.0, [fy[i, j] for j in range(8)], -1)
        for j in range(8):
            gy[i, j] = line[j]

    for i, j in deep:
        first_step(i, j, load_v[i, :, j, :], dg[i, j])

    def z_part(at):
        shape = fs[at].shape
        flux = wide_dot(fs[at].reshape(-1, 128), mats[0]) * fz[at].reshape(-1, 128)
        zz[at] = wide_dot(flux, mats[1]).reshape(shape)

    def column(line, m, n):
        return total([float(DERIV[a, m] * DERIV[a, n]) * line[a] for a in range(8)])

    z_part((slice(1, 7), slice(1, 7)))
    for j in inner:
        grad = apply_line(DERIV, [None] + [fs[i, j] for i in inner] + [None], -1)
        line = apply_line(DERIV.T, [fx[i, j] * grad[i] for i in range(8)], -1)
        for i in range(8):
            kv[i, j] = line[i]
        line = [fx[a, j] for a in range(8)]
        for i in range(8):
            k0[i, j] = column(line, i, 0)
    for i in inner:
        grad = apply_line(DERIV, [None] + [fs[i, j] for j in inner] + [None], -1)
        line = apply_line(DERIV.T, [fy[i, j] * grad[j] for j in range(8)], -1)
        for j in range(8):
            kv[i, j] = (kv[i, j] + (line[j] + zz[i, j])) if j in inner else line[j]
        line = [fy[i, b] for b in range(8)]
        for j in range(8):
            ky0[i, j] = column(line, j, 0)
            ky7[i, j] = column(line, j, 7)

    def low_high(v):
        plain = total(v)
        slope = total([float(NODES[m]) * (v[m] - v[7 - m]) for m in range(4)])
        return (plain - slope) * 0.125, (plain + slope) * 0.125

    held = [low_high([load_v[i, :, j, :] for i in range(8)]) for j in range(8)]
    held = [low_high([held[j][p] for j in range(8)]) for p in range(2)]
    for p in range(2):
        for q in range(2):
            hold[2 * p + q] = held[p][q]

    wide = lambda row: jnp.broadcast_to(row, (8, 128))

    def start_rim(planes_i):
        loads = rim_sums(
            planes_i,
            lambda i, j: load_v[i, :, j, :],
            lambda side, j: rxl[side, :, j, :],
            lambda side, i: wide(rya[side, 0, i : i + 1, :]),
            lambda slot, i: wide(rca[slot, 0:1, :]),
        )
        diags = rim_sums(
            planes_i,
            lambda i, j: dg[i, j],
            lambda side, j: rxd[side, j],
            lambda side, i: wide(rya[side, 1, i : i + 1, :]),
            lambda slot, i: wide(rca[slot, 1:2, :]),
        )
        for i, j in loads:
            first_step(i, j, loads[i, j], diags[i, j])

    for n in (4, 5, 6, 8, 0, 1):
        first[n].wait_recv()
    start_rim(range(7))
    for j in range(8):
        if j in inner:
            v = fs[0, j]
            for i in range(8):
                kv[i, j] = kv[i, j] + k0[i, j] * v
        else:
            grad = apply_line(DERIV, [fs[i, j] for i in range(7)] + [None], -1)
            line = apply_line(DERIV.T, [fx[i, j] * grad[i] for i in range(8)], -1)
            for i in range(8):
                kv[i, j] = (kv[i, j] + line[i]) if i in inner else line[i]
    sye[0] = kv[:, 7, 7, :]
    sye[1] = kv[:, 0, 0, :]
    second = [
        send(sye.at[0], rcb.at[0], (dn, sn)),
        send(sye.at[1], rcb.at[1], (dn, sp)),
        send(kv.at[7], rxb.at[0], (dn, s)),
    ]

    z_part((slice(1, 7), 0))
    z_part((slice(1, 7), 7))
    for i in inner:
        low, high = fs[i, 0], fs[i, 7]
        for j in range(8):
            value = kv[i, j] + (ky0[i, j] * low + ky7[i, j] * high)
            kv[i, j] = value if j in inner else value + zz[i, j]
    first[10].wait_recv()
    for j in range(8):
        fy[0, j] = fy[0, j] + rxg[j] * rxg[8]
        fz[0, j] = fz[0, j] + rxg[j] * rxg[9]
    z_part(slice(0, 1))
    grad = apply_line(DERIV, [fs[0, j] for j in range(8)], -1)
    line = apply_line(DERIV.T, [fy[0, j] * grad[j] for j in range(8)], -1)
    for j in range(8):
        kv[0, j] = kv[0, j] + rxg[10 + j] * fs[0, j] + (line[j] + zz[0, j])
    syb[0] = kv[:, 7, 7, :]
    syb[1] = kv[:, 0, 0, :]
    second += [send(syb.at[0], ryb.at[0], (d, sn)), send(syb.at[1], ryb.at[1], (d, sp))]

    for n in (2, 3, 7, 9):
        first[n].wait_recv()
    start_rim((7,))
    for j in range(8):
        v = fs[7, j]
        for i in range(7):
            kv[i, j] = kv[i, j] + k7[i, j] * v
    syc[0] = kv[:, 7, 7, :]
    syc[1] = kv[:, 0, 0, :]
    second += [
        send(syc.at[0], rcb.at[2], (dp, sn)),
        send(syc.at[1], rcb.at[3], (dp, sp)),
        send(kv.at[0], rxb.at[1], (dp, s)),
    ]
    gz[0] = wide_dot(fz[0].reshape(64, 128), mats[1]).reshape(8, 8, 128)
    line = apply_line(DERIV.T / 8.0, [fy[0, j] for j in range(8)], -1)
    for j in range(8):
        gy[0, j] = line[j]
    for n in (11, 12):
        first[n].wait_recv()
    ends = [fs[7, 0], fs[7, 7]]

    weight = [[float((1.0 + (2 * p - 1) * NODES[m]) / 8.0) for m in range(8)] for p in range(2)]
    part_x, part_y, part_z = [[] for _ in range(8)], [[] for _ in range(8)], {}

    def smoothed(i, j, value):
        resid = rhs[i, j] - z_joined(value)
        p = KEEP * fs[i, j] + STEP * (inv[i, j] * resid)
        fs[i, j] = p
        press_ref[0, i, :, j, :] = p

    for i, j in deep:
        smoothed(i, j, kv[i, j])

    def finish(planes_i):
        sums = rim_sums(
            planes_i,
            lambda i, j: kv[i, j],
            lambda side, j: rxb[side, j],
            lambda side, i: wide(ryb[side, i : i + 1, :])
            + (wide(rk[side, i : i + 1, :]) * ends[side] if i < 7 else 0.0),
            lambda slot, i: wide(rcb[slot, i : i + 1, :]),
        )
        for (i, j), value in sums.items():
            smoothed(i, j, value)

    def weigh(line, p):
        return total([weight[p][m] * v for m, v in enumerate(line) if weight[p][m] != 0.0])

    def vertices(plain, cells):
        both = wide_dot(jnp.concatenate(plain, axis=0), mats[3]) + wide_dot(
            jnp.concatenate(cells, axis=0), mats[4]
        )
        inside, edge = both[0:8], pltpu.roll(both[8:16], 1, 0)
        return inside + jnp.where(sub8 == 0, 0.0, edge), jnp.where(sub8 == 0, edge, 0.0)

    x_deep = {j: total([gx[i, j] * fs[i, j] for i in inner]) for j in inner}
    y_deep = {i: total([gy[i, j] * fs[i, j] for j in inner]) for i in inner}
    z_deep = {}
    for i in inner:
        terms = {j: gz[i, j] * fs[i, j] for j in inner}
        z_deep[i] = [total([weight[q][j] * v for j, v in terms.items()]) for q in range(2)]
    for n in (2, 0, 1, 3, 4):
        second[n].wait_recv()
    finish(range(7))
    x_sum, y_sum, z_line = [], [], []
    for j in range(8):
        deep_part = x_deep[j] if j in inner else total([gx[i, j] * fs[i, j] for i in inner])
        x_sum.append(deep_part + gx[0, j] * fs[0, j])
    for i in range(7):
        if i in inner:
            low, high = gz[i, 0] * fs[i, 0], gz[i, 7] * fs[i, 7]
            y_sum.append(y_deep[i] + (gy[i, 0] * fs[i, 0] + gy[i, 7] * fs[i, 7]))
            z_line.append([z_deep[i][0] + 0.25 * low, z_deep[i][1] + 0.25 * high])
        else:
            y_sum.append(total([gy[i, j] * fs[i, j] for j in range(8)]))
            terms = [gz[i, j] * fs[i, j] for j in range(8)]
            z_line.append([weigh(terms, q) for q in range(2)])
    y_high = weigh(y_sum, 1)
    plain = [
        hold[2] - weigh(x_sum, 0) + y_high,
        hold[3] - weigh(x_sum, 1) - y_high,
    ]
    cells = [-weigh([z[q] for z in z_line], 1) for q in range(2)]
    sc[0], sc[1] = vertices(plain, cells)
    third = [
        send(sc.at[1], rc.at[1], (dn, sn)),
        send(sc.at[0], rc.at[0], (dn, s)),
    ]
    for n in (5, 6, 7):
        second[n].wait_recv()
    finish((7,))
    first[13].wait_recv()
    x_net = [x_sum[j] + gx[7, j] * fs[7, j] - rxgx[j] * fs[0, j] for j in range(8)]
    y_low = weigh(y_sum + [y_sum[0]], 0)
    plain = [
        hold[0] + weigh(x_net, 0) + y_low,
        hold[1] + weigh(x_net, 1) - y_low,
    ]
    cells = [-weigh([z[q] for z in z_line] + [z_line[0][q]], 0) for q in range(2)]
    own, sc[2] = vertices(plain, cells)
    third.append(send(sc.at[2], rc.at[2], (d, sn)))
    for copy in third:
        copy.wait_recv()
    coarse = own + rc[0] + (rc[1] + rc[2])
    coarse_ref[0] = coarse[:, 0:17]
    for copy in first + second + third:
        copy.wait_send()


def write_out(pressure_ref, coarse_ref, pressure_hbm, coarse_hbm, sem):
    copies = [pltpu.make_async_copy(coarse_ref, coarse_hbm, sem.at[8])]
    copies += [
        pltpu.make_async_copy(pressure_ref.at[0, i], pressure_hbm.at[0, i], sem.at[i])
        for i in range(8)
    ]
    for copy in copies:
        copy.start()
    for copy in copies:
        copy.wait()


def shards(element_load, mobility, metric):
    field = pltpu.VMEM((8, 8, 8, 128), F32)
    hbm = pl.BlockSpec(memory_space=pltpu.HBM)
    vmem = pl.BlockSpec(memory_space=pltpu.VMEM)
    pressure, coarse = pl.pallas_call(
        kernel,
        name="smoother",
        out_shape=(
            pltpu.VMEM((1, 8, 8, 8, 128), F32),
            pltpu.VMEM((1, 8, 17), F32),
        ),
        in_specs=[hbm, hbm, hbm, hbm],
        out_specs=(vmem, vmem),
        scratch_shapes=[
            field, field,
            pltpu.VMEM((3, 1, 8, 16), F32),
            pltpu.VMEM((5, 8, 128), F32),
            pltpu.VMEM((5, 256, 256), BF16),
            *[field] * 16,
            pltpu.VMEM((4, 8, 128), F32),
            pltpu.VMEM((2, 2, 8, 128), F32),
            pltpu.VMEM((4, 2, 128), F32),
            pltpu.VMEM((18, 8, 128), F32),
            pltpu.VMEM((8, 8, 128), F32),
            pltpu.VMEM((2, 8, 128), F32),
            pltpu.VMEM((2, 8, 128), F32),
            pltpu.VMEM((2, 8, 128), F32),
            pltpu.VMEM((2, 8, 128), F32),
            pltpu.VMEM((3, 8, 128), F32),
            pltpu.VMEM((2, 8, 8, 128), F32),
            pltpu.VMEM((2, 8, 8, 128), F32),
            pltpu.VMEM((18, 8, 128), F32),
            pltpu.VMEM((8, 8, 128), F32),
            pltpu.VMEM((2, 2, 8, 128), F32),
            pltpu.VMEM((4, 2, 128), F32),
            pltpu.VMEM((2, 8, 128), F32),
            pltpu.VMEM((2, 8, 8, 128), F32),
            pltpu.VMEM((2, 8, 128), F32),
            pltpu.VMEM((4, 8, 128), F32),
            pltpu.VMEM((3, 8, 128), F32),
            pltpu.SemaphoreType.DMA((5,)),
            pltpu.SemaphoreType.DMA((25,)),
            pltpu.SemaphoreType.DMA((25,)),
        ],
        compiler_params=pltpu.CompilerParams(collective_id=0, has_side_effects=True),
    )(element_load, mobility, metric, jnp.asarray(small_tables()))
    return pl.pallas_call(
        write_out,
        name="write_out",
        out_shape=(
            jax.ShapeDtypeStruct(pressure.shape, F32),
            jax.ShapeDtypeStruct(coarse.shape, F32),
        ),
        in_specs=[vmem, vmem],
        out_specs=(hbm, hbm),
        scratch_shapes=[pltpu.SemaphoreType.DMA((9,))],
    )(
        pltpu.with_memory_space_constraint(pressure, pltpu.VMEM),
        pltpu.with_memory_space_constraint(coarse, pltpu.VMEM),
    )


def solution(mesh):
    in_specs = (
        P("dom", None, "sub", None, None),
        P("dom", None, "sub", None, None),
        P(None, "dom", "sub", None),
    )
    out_specs = (P("dom", None, "sub", None, None), P("dom", "sub", None))
    return jax.shard_map(shards, mesh=mesh, in_specs=in_specs, out_specs=out_specs, check_vma=False)
```
